128 devices in a mesh: dp: 4 (over z), latent: 32 (over x, y, core).
Axes of the slice: x: 4, y: 4, z: 4, core: 2. Of those that a mesh axis runs over, the one named last changes fastest.
Arguments:
- acts: bfloat16 [640, 8192], P(('dp', 'latent')), may hold values from -6 to 6
- chat_len: int32 [128], P(('dp', 'latent')), may hold values from 1 to 5, as said below
- group_of: int32 [640, 1], P(('dp', 'latent')), may hold values from 0 to 4; in each aligned block of 5 rows (0 to 4, 5 to 9, ...) no two rows name the same one
- w_enc: bfloat16 [2, 4096, 16384], P(None, None, 'latent'), may hold values from -0.0625 to 0.0625
- b_enc: float32 [16384], P('latent'), may hold values from -3 to 3
- w_dec: bfloat16 [16384, 8192], P('latent'), may hold values from -0.046875 to 0.046875
- b_dec: float32 [2, 4096], replicated, may hold values from -3 to 3
Outputs:
- grad_enc: bfloat16 [2, 4096, 16384], P(None, 'dp', 'latent')
- grad_dec: bfloat16 [16384, 8192], P('latent', 'dp')
- loss: float32 [], replicated
The draws below stay inside these ranges and needn't reach their ends.
Inputs may be any that keep to these rules, and one draw needn't show every extreme that they name: `chat_len`: the last serving shard harvests all 5 rows. `group_of`: among the 5 row slots of each serving shard every value 0 to 4 appears exactly once.
All inputs are finite; a program needn't handle non-finite values.
Results may differ from the reference program's by a relative error of at most 0.02.
Values may be sent and summed in bfloat16 or wider, within the bound.
No kernel may reach another device: no remote copies, remote signals or barrier semaphores. Data moves between devices by JAX's collectives and lax.ppermute only.
A program may use at most 128 MiB of HBM per device.

```python
import math
import jax
import jax.numpy as jnp
import numpy as np
from jax import lax

D = 4096
CAP = 1
LATENTS = 16384
SLOTS = 5
ROWS_IN = 640
GROUP_ROWS = 128
N_DP = 4
DEVICES = 128


def draw_chat_len(key, part):
    index = jnp.arange(DEVICES, dtype=jnp.int32)
    span = max(DEVICES - 1, 1)
    base = (SLOTS * span + 2 * SLOTS * index) // (3 * span)
    jitter = jax.random.randint(key, (DEVICES,), -1, 2, dtype=jnp.int32)
    length = jnp.clip(base + jitter, 1, SLOTS)
    return jnp.where(index == DEVICES - 1, SLOTS, length).astype(jnp.int32)


def steps_of(stream_key, shape, shards, low, high):
    factor_of, own = 1.0, jax.random.fold_in(stream_key, 6)
    for axis_at, parts in shards:
        draws = jnp.exp(jax.random.uniform(jax.random.fold_in(own, axis_at), (parts,), jnp.float32, low / len(shards), high / len(shards)))
        factor_of = factor_of * jnp.repeat(draws, shape[axis_at] // parts).reshape([-1 if axis == axis_at else 1 for axis in range(len(shape))])
    return factor_of


def shared_out(stream_key, own, number, rows, count, top, limit, slope):
    sequence = jax.random.permutation(stream_key, count)
    heavy_load, common = shares(count, rows * top, limit, slope, True), shares(count, rows * top, limit, slope, False)
    places = jnp.arange(count)

    def named(lengths, rotation):
        used = int((lengths > 0).sum())
        fixed = max(1, used // 4)
        shifted = fixed + (places - fixed + rotation * (used - fixed)) % max(1, count - fixed)
        return jnp.zeros((count,), jnp.int32).at[sequence[jnp.where(places < fixed, places, shifted)]].set(jnp.asarray(lengths, jnp.int32))

    lengths = jnp.where(number % 4 == 0, named(heavy_load, number // 4), named(common, number - number // 4 - 1))
    mixed = jax.random.permutation(jax.random.fold_in(own, 3), count)
    source_of, receiver = mixed[0:count // 2 * 2:2], mixed[1:count // 2 * 2:2]
    margin = jnp.minimum(lengths[source_of] - 1, limit - lengths[receiver]) // 2
    margin = jnp.where((source_of == sequence[0]) | (receiver == sequence[0]) | (lengths[receiver] == 0), 0, jnp.maximum(margin, 0))
    shifted = jax.random.randint(jax.random.fold_in(own, 4), (count // 2,), 0, 1 << 20) % (margin + 1)
    lengths = lengths.at[source_of].add(-shifted).at[receiver].add(shifted)
    items = jnp.searchsorted(jnp.cumsum(lengths), jnp.arange(rows * top), side="right").astype(jnp.int32)
    listing = items.reshape(top, rows).T
    listing = listing[jax.random.permutation(jax.random.fold_in(own, 1), rows)]
    rotation = jax.random.randint(jax.random.fold_in(own, 2), (rows, 1), 0, top)
    return jnp.take_along_axis(listing, (jnp.arange(top)[None, :] + rotation) % top, axis=1)


def shares(amount, total, reach, lean, full):
    portions = [(1 << 20) // math.isqrt(grade ** lean) + 1 for grade in range(1, amount + 1)]
    largest = reach if full else min(reach, max(-(-total // amount), total * portions[0] // sum(portions)))
    least = 1 if total - largest >= amount - 1 else 0
    counts, spare = [largest] + [least] * (amount - 1), total - largest - least * (amount - 1)
    while spare > 0:
        candidates = [i for i in range(1, amount) if counts[i] < largest] or [i for i in range(1, amount) if counts[i] < reach]
        whole, budget = sum([portions[i] for i in candidates]), spare
        for i in candidates:
            addition = min(reach - counts[i], max(1, budget * portions[i] // whole), spare)
            counts[i] = counts[i] + addition
            spare = spare - addition
    return np.array(counts)


def gaussian(key, extent, scale, most, split=(), held_as=jnp.bfloat16):
    drawn = scale * jax.random.normal(key, extent, jnp.float32)
    if split:
        drawn = drawn * steps_of(key, extent, split, -0.22, 0.18)
    return jnp.clip(drawn, -most, most).astype(held_as)


def setup_inputs(seed: int = 0) -> dict:
    seeds = jax.random.split(jax.random.key(seed), 8)
    acts = gaussian(seeds[0], (ROWS_IN, 2 * D), 1.0, 6.0, ((0, 128),))
    chat_len = draw_chat_len(jax.random.fold_in(seeds[7], 71), 0)
    group_of_keys = jax.random.split(jax.random.fold_in(seeds[2], 1), ROWS_IN // SLOTS)
    group_of_turns = jax.random.permutation(jax.random.fold_in(seeds[2], 3), ROWS_IN // SLOTS)
    group_of = jax.vmap(lambda own, number: shared_out(jax.random.fold_in(seeds[2], 2), own, number, SLOTS, N_DP + 1, 1, CAP, 0))(group_of_keys, group_of_turns).reshape((ROWS_IN, 1))
    w_enc = gaussian(seeds[3], (2, D, LATENTS), (2 * D) ** -0.5, 0.0625, ((2, 32),))
    b_enc = gaussian(seeds[4], (LATENTS,), 0.5, 3.0, ((0, 32),), jnp.float32)
    w_dec = gaussian(seeds[5], (LATENTS, 2 * D), LATENTS ** -0.5, 0.046875, ((0, 32),))
    b_dec = gaussian(seeds[6], (2, D), 0.5, 3.0, (), jnp.float32)
    return {"acts": acts, "chat_len": chat_len, "group_of": group_of, "w_enc": w_enc, "b_enc": b_enc, "w_dec": w_dec, "b_dec": b_dec}


sparsity_weight = 1.0
loss_scale = 8.0
norm_eps = 1e-06

def reference(acts, chat_len, group_of, w_enc, b_enc, w_dec, b_dec):
    width = 2 * D
    rows = acts.shape[0]
    slot_ids = jnp.arange(rows, dtype=jnp.int32)
    owner = (slot_ids // SLOTS).astype(jnp.int32)
    alive = (slot_ids % SLOTS < chat_len[owner]).astype(jnp.float32)
    order = jnp.argsort(group_of[:, 0], stable=True).astype(jnp.int32)
    kept = order[:N_DP * GROUP_ROWS]
    grouped = acts[kept].reshape(N_DP, GROUP_ROWS, width)
    masks = alive[kept].reshape(N_DP, GROUP_ROWS)
    count = jnp.sum(masks)
    wenc_flat = w_enc.reshape(width, LATENTS)
    squares_dec = jnp.square(w_dec.astype(jnp.float32))
    norm_base = jnp.sqrt(lax.optimization_barrier(jnp.sum(squares_dec[:, :D], axis=1)) + norm_eps)
    norm_inst = jnp.sqrt(lax.optimization_barrier(jnp.sum(squares_dec[:, D:], axis=1)) + norm_eps)
    norm_sum = norm_base + norm_inst
    column_ids = jnp.arange(width, dtype=jnp.int32)
    bias_row = b_dec.reshape(width)

    def step(carry, item):
        enc_acc, dec_acc, loss_acc = carry
        xg, maskg = item
        pre = jnp.dot(xg, wenc_flat, preferred_element_type=jnp.float32) + b_enc[None, :]
        act = jnp.maximum(pre, 0.0)
        feats = act * act
        feats16 = feats.astype(jnp.bfloat16)
        recon = jnp.dot(feats16, w_dec, preferred_element_type=jnp.float32)
        err = (recon + bias_row[None, :] - xg.astype(jnp.float32)) * maskg[:, None]
        err16 = err.astype(jnp.bfloat16)
        fsum = lax.optimization_barrier(jnp.sum(feats * maskg[:, None], axis=0))
        part_loss = jnp.sum(err * err) + sparsity_weight * jnp.sum(fsum * norm_sum)
        dfeat = 2.0 * lax.dot_general(err16, w_dec, (((1,), (1,)), ((), ())), preferred_element_type=jnp.float32)
        dfeat = dfeat + sparsity_weight * maskg[:, None] * norm_sum[None, :]
        dpre16 = (dfeat * 2.0 * act).astype(jnp.bfloat16)
        enc_term = lax.dot_general(xg, dpre16, (((0,), (0,)), ((), ())), preferred_element_type=jnp.float32)
        dec_term = 2.0 * lax.dot_general(feats16, err16, (((0,), (0,)), ((), ())), preferred_element_type=jnp.float32)
        scale = jnp.where(column_ids[None, :] < D, (fsum / norm_base)[:, None], (fsum / norm_inst)[:, None])
        dec_term = dec_term + sparsity_weight * scale * w_dec.astype(jnp.float32)
        enc_round = lax.optimization_barrier(enc_term.astype(jnp.bfloat16))
        dec_round = lax.optimization_barrier(dec_term.astype(jnp.bfloat16))
        enc_acc = enc_acc + enc_round.astype(jnp.float32)
        dec_acc = dec_acc + dec_round.astype(jnp.float32)
        return ((enc_acc, dec_acc, loss_acc + part_loss), None)
    start = (jnp.zeros((width, LATENTS), jnp.float32), jnp.zeros((LATENTS, width), jnp.float32), jnp.zeros((), jnp.float32))
    (enc_acc, dec_acc, total), _ = lax.scan(step, start, (grouped, masks))
    factor = loss_scale / count
    grad_enc = (enc_acc * factor).astype(jnp.bfloat16).reshape(2, D, LATENTS)
    grad_dec = (dec_acc * factor).astype(jnp.bfloat16)
    loss = total / (count * width)
    return (grad_enc, grad_dec, loss)
```

```python
import jax
import jax.numpy as jnp
from jax import lax
from jax.experimental import pallas as pl
from jax.experimental.pallas import tpu as pltpu
from jax.sharding import Mesh
from jax.sharding import PartitionSpec as P

sparsity_weight = 1.0
loss_scale = 8.0
norm_eps = 1e-06

ALL = ("z", "x", "y", "c")
NZ = 4
CHIPS = 16
WIDTH = 8192
HALF = 4096
SUB = 1024
LOCAL = 512
ROWS = 128
PAD = 128
MIB = 1 << 20
f32 = jnp.float32
bf16 = jnp.bfloat16

VM = pl.BlockSpec(memory_space=pltpu.VMEM)
SM = pl.BlockSpec(memory_space=pltpu.SMEM)


def call(body, outs, args, specs=None, scratch=(), vmem=None, flops=0, nbytes=0):
    return pl.pallas_call(
        body,
        out_shape=[jax.ShapeDtypeStruct(s, d) for s, d in outs],
        in_specs=specs or [VM] * len(args),
        out_specs=[VM] * len(outs),
        scratch_shapes=list(scratch),
        compiler_params=pltpu.CompilerParams(vmem_limit_bytes=vmem or 24 * MIB),
        cost_estimate=pl.CostEstimate(flops=flops, bytes_accessed=nbytes, transcendentals=0),
    )(*args)


def lanes(start, size):
    return pl.ds(pl.multiple_of(start, 128), size)


def split3(v):
    hi = v.astype(bf16)
    rest = v - hi.astype(f32)
    mid = rest.astype(bf16)
    low = (rest - mid.astype(f32)).astype(bf16)
    return hi, mid, low


def prep_kernel(who, length, acts, group, keep, send):
    c = who[1]
    slot = lax.broadcasted_iota(jnp.int32, (5, 1), 0)
    held = jnp.sum(jnp.where(group[...] == NZ, slot, 0), axis=0, keepdims=True)
    k = lax.broadcasted_iota(jnp.int32, (4, 1), 0)
    later = k >= held
    src = k + later.astype(jnp.int32)
    live = (src < length[0]).astype(f32)
    live = jnp.broadcast_to(live, (4, PAD)).astype(bf16)

    def pick(cols):
        rows = acts[:, cols].astype(f32)
        return jnp.where(later, rows[1:5], rows[0:4]).astype(bf16)

    for out, core in ((keep, c), (send, 1 - c)):
        out[:, :HALF] = pick(lanes(core * HALF, HALF))
        for q in range(NZ):
            out[:, HALF + q * SUB : HALF + (q + 1) * SUB] = pick(lanes(q * 2 * SUB + core * SUB, SUB))
        out[:, 2 * HALF :] = live


def join_kernel(who, own, other, out, mine):
    first = who[1] == 0
    a, b = own[...].astype(f32), other[...].astype(f32)
    rows = jnp.concatenate([jnp.where(first, a, b), jnp.where(first, b, a)], axis=0)
    mine[...] = rows[:, HALF:].astype(bf16)
    for i in range(CHIPS):
        out[i, :, :HALF] = rows[:, :HALF].astype(bf16)
        out[i, :, HALF:] = rows[:, 2 * HALF :].astype(bf16)


def encode_own_kernel(who, x, w_enc, acc, *slices):
    z, c = who[0], who[1]
    for n in range(0, LOCAL, 256):
        acc[:, n : n + 256] = jnp.dot(x[:, :HALF], w_enc[c, :, n : n + 256], preferred_element_type=f32)
    for k in range(NZ):
        dest = lax.rem(z + k, NZ)
        slices[k][...] = x[:, lanes(dest * SUB, SUB)]


def encode_kernel(who, x, w_enc, acc, bias, w_dec, act_out, feats_out, send):
    c = who[1]
    for n in range(0, LOCAL, 256):
        pre = acc[:, n : n + 256] + jnp.dot(
            x[:, :HALF], w_enc[1 - c, :, n : n + 256], preferred_element_type=f32
        )
        act = jnp.maximum(pre + bias[:, n : n + 256], 0.0)
        feats = act * act
        act_out[:, n : n + 256] = act
        feats_out[:ROWS, n : n + 256] = feats.astype(bf16)
        live = x[:, HALF : HALF + 1].astype(f32)
        fsum = jnp.sum(feats * live, axis=0, keepdims=True)
        hi, mid, low = split3(fsum)
        row = lax.broadcasted_iota(jnp.int32, (16, 256), 0)
        tail = jnp.where(row == 0, hi.astype(f32), jnp.where(row == 1, mid.astype(f32), low.astype(f32)))
        feats_out[ROWS:, n : n + 256] = jnp.where(row < 3, tail, 0.0).astype(bf16)
    feats16 = feats_out[:ROWS, :]
    for q in range(NZ):
        cols = lanes(q * 2 * SUB + (1 - c) * SUB, SUB)
        send[:, q * SUB : (q + 1) * SUB] = jnp.dot(feats16, w_dec[:, cols], preferred_element_type=f32).astype(bf16)


def decode_own_kernel(who, feats, w_dec, part, norm_rows, norm_cols):
    c = who[1]
    feats16 = feats[:ROWS, :]
    for q in range(NZ):
        cols = lanes(q * 2 * SUB + c * SUB, SUB)
        part[:, q * SUB : (q + 1) * SUB] = jnp.dot(feats16, w_dec[:, cols], preferred_element_type=f32)
    for s in range(2):
        for n in range(0, LOCAL, 128):
            def add(i, total):
                v = w_dec[n : n + 128, lanes(s * HALF + i * 256, 256)].astype(f32)
                v = v * v
                return total + v[:, :128] + v[:, 128:]

            total = lax.fori_loop(0, HALF // 256, add, jnp.zeros((128, 128), f32))
            norm_rows[s : s + 1, n : n + 128] = jnp.sqrt(jnp.sum(total.T, axis=0, keepdims=True) + norm_eps)
            norm_cols[n : n + 128, s : s + 1] = jnp.sqrt(jnp.sum(total, axis=1, keepdims=True) + norm_eps)


def add_kernel(own, other, out):
    for n in range(0, HALF, SUB):
        out[:, n : n + SUB] = (own[:, n : n + SUB] + other[:, n : n + SUB].astype(f32)).astype(bf16)


def err_kernel(who, parts, mine, bias, feats, norm_rows, out):
    c = who[1]
    live = mine[:, HALF : HALF + 1].astype(f32)
    square = jnp.zeros((8, SUB), f32)
    for q in range(NZ):
        cols = slice(q * SUB, (q + 1) * SUB)
        total = parts[0, :, cols].astype(f32)
        for i in range(1, CHIPS):
            total = total + parts[i, :, cols].astype(f32)
        add = bias[q // 2 : q // 2 + 1, lanes((q % 2) * 2 * SUB + c * SUB, SUB)]
        err = (total + add - mine[:, cols].astype(f32)) * live
        square = square + err * err
        err16 = err.astype(bf16)
        for i in range(CHIPS):
            out[i, :, cols] = err16
    squares = jnp.sum(jnp.sum(square, axis=0, keepdims=True), axis=1, keepdims=True)
    fsum = jnp.sum(feats[ROWS : ROWS + 16, :].astype(f32), axis=0, keepdims=True)
    nsum = norm_rows[0:1, :] + norm_rows[1:2, :]
    sparse = sparsity_weight * jnp.sum(fsum * nsum, axis=1, keepdims=True)
    hi, mid, low = split3(squares + sparse)
    lane = lax.broadcasted_iota(jnp.int32, (8, PAD), 1)
    row = lax.broadcasted_iota(jnp.int32, (8, PAD), 0)
    tail = jnp.where(lane == 0, hi.astype(f32), jnp.where(lane == 1, mid.astype(f32), low.astype(f32)))
    tail = jnp.where((row == 0) & (lane < 3), tail, 0.0).astype(bf16)
    for i in range(CHIPS):
        out[i, :, HALF:] = tail


def dfeat_own_kernel(who, e, w_dec, acc, *slices):
    z, c = who[0], who[1]
    for n in range(0, LOCAL, 256):
        total = jnp.zeros((ROWS, 256), f32)
        for q in range(NZ):
            w = w_dec[n : n + 256, lanes(q * 2 * SUB + c * SUB, SUB)]
            total = total + lax.dot_general(
                e[:, q * SUB : (q + 1) * SUB], w, (((1,), (1,)), ((), ())), preferred_element_type=f32
            )
        acc[:, n : n + 256] = total
    for k in range(NZ):
        dest = lax.rem(z + k, NZ)
        slices[k][...] = e[:, lanes(dest * SUB, SUB)]


def dpre_kernel(who, e, own, w_dec, acc, act, x, norm_rows, out):
    c = who[1]
    live = x[:, HALF : HALF + 1].astype(f32)
    for n in range(0, LOCAL, 256):
        total = acc[:, n : n + 256]
        for q in range(NZ):
            w = w_dec[n : n + 256, lanes(q * 2 * SUB + (1 - c) * SUB, SUB)]
            total = total + lax.dot_general(
                e[:, q * SUB : (q + 1) * SUB], w, (((1,), (1,)), ((), ())), preferred_element_type=f32
            )
        nsum = norm_rows[0:1, n : n + 256] + norm_rows[1:2, n : n + 256]
        dfeat = 2.0 * total + sparsity_weight * live * nsum
        out[:ROWS, n : n + 256] = (dfeat * 2.0 * act[:, n : n + 256]).astype(bf16)
    tail = e[:, HALF:].astype(f32) + own[:, HALF:].astype(f32)
    both = jnp.sum(jnp.sum(e[:, HALF:].astype(f32), axis=0, keepdims=True), axis=1, keepdims=True)
    both = both + jnp.sum(jnp.sum(own[:, HALF:].astype(f32), axis=0, keepdims=True), axis=1, keepdims=True)
    del tail
    count = jnp.sum(live, axis=0, keepdims=True)
    hi, mid, low = split3(both)
    lane = lax.broadcasted_iota(jnp.int32, (16, LOCAL), 1)
    row = lax.broadcasted_iota(jnp.int32, (16, LOCAL), 0)
    tail = jnp.where(
        lane == 0,
        hi.astype(f32),
        jnp.where(lane == 1, mid.astype(f32), jnp.where(lane == 2, low.astype(f32), count)),
    )
    out[ROWS:, :] = jnp.where((row == 0) & (lane < 4), tail, 0.0).astype(bf16)


def totals(pres):
    total = jnp.zeros((1, 1), f32)
    count = jnp.zeros((1, 1), f32)
    for p in pres:
        row = p[ROWS : ROWS + 1, 0:PAD].astype(f32)
        lane = lax.broadcasted_iota(jnp.int32, (1, PAD), 1)
        total = total + jnp.sum(jnp.where(lane < 3, row, 0.0), axis=1, keepdims=True)
        count = count + jnp.sum(jnp.where(lane == 3, row, 0.0), axis=1, keepdims=True)
    return total, count


def grad_enc_kernel(who, *refs):
    c = who[1]
    own, other, pres = refs[0:4], refs[4:8], refs[8:12]
    out, loss, xs, ds = refs[12:]
    total, count = totals(pres)
    loss[...] = total / (count * WIDTH)
    factor = loss_scale / count
    for k in range(NZ):
        ds[k * ROWS : (k + 1) * ROWS, :] = pres[k][:ROWS, :]
    for side, group in ((c, own), (1 - c, other)):
        for k in range(NZ):
            xs[k * ROWS : (k + 1) * ROWS, :] = group[k][...]
        for n in range(0, SUB, 256):
            part = lax.dot_general(
                xs[:, n : n + 256], ds[...], (((0,), (0,)), ((), ())), preferred_element_type=f32
            )
            out[side, n : n + 256, :] = (part * factor).astype(bf16)


def grad_dec_kernel(who, *refs):
    z, c = who[0], who[1]
    own, other, feats, pres = refs[0:4], refs[4:8], refs[8:12], refs[12:16]
    norm_cols, w_dec, out, es, fs = refs[16:]
    _, count = totals(pres)
    factor = loss_scale / count
    fsum = jnp.zeros((16, LOCAL), f32)
    for k in range(NZ):
        fs[k * ROWS : (k + 1) * ROWS, :] = feats[k][:ROWS, :]
        fsum = fsum + feats[k][ROWS:, :].astype(f32)
    fsum = jnp.sum(jnp.broadcast_to(jnp.sum(fsum, axis=0, keepdims=True), (128, LOCAL)).T, axis=1, keepdims=True) * (1.0 / 128.0)
    norm = jnp.where(z < 2, norm_cols[:, 0:1], norm_cols[:, 1:2])
    scale = sparsity_weight * fsum / norm
    for side, group in ((c, own), (1 - c, other)):
        for k in range(NZ):
            es[k * ROWS : (k + 1) * ROWS, :] = group[k][...]
        for n in range(0, LOCAL, 256):
            part = 2.0 * lax.dot_general(
                fs[:, n : n + 256], es[...], (((0,), (0,)), ((), ())), preferred_element_type=f32
            )
            w = w_dec[n : n + 256, lanes(z * 2 * SUB + side * SUB, SUB)].astype(f32)
            part = part + scale[n : n + 256, :] * w
            out[n : n + 256, lanes(side * SUB, SUB)] = (part * factor).astype(bf16)


def swap(v):
    return lax.ppermute(v, "c", [(0, 1), (1, 0)])


def shift(v, k):
    return lax.ppermute(v, "z", [(i, (i + k) % NZ) for i in range(NZ)])


def shards(acts, chat_len, group_of, w_enc, b_enc, w_dec, b_dec):
    who = jnp.stack([lax.axis_index("z"), lax.axis_index("c")]).astype(jnp.int32)
    keep, send = call(
        prep_kernel,
        [((4, 2 * HALF + PAD), bf16)] * 2,
        (who, chat_len, acts, group_of),
        [SM, SM, VM, VM],
    )
    block, mine = call(
        join_kernel,
        [((CHIPS, 8, HALF + PAD), bf16), ((8, HALF + PAD), bf16)],
        (who, keep, swap(send)),
        [SM, VM, VM],
    )
    x_own = lax.all_to_all(block, ("x", "y"), split_axis=0, concat_axis=0, tiled=True).reshape(ROWS, HALF + PAD)
    x_other = swap(x_own)
    acc, *x_slices = call(
        encode_own_kernel,
        [((ROWS, LOCAL), f32)] + [((ROWS, SUB), bf16)] * NZ,
        (who, x_own, w_enc),
        [SM, VM, VM],
        flops=2 * ROWS * HALF * LOCAL,
        nbytes=6 * MIB,
    )
    act, feats, part_send = call(
        encode_kernel,
        [((ROWS, LOCAL), f32), ((ROWS + 16, LOCAL), bf16), ((ROWS, HALF), bf16)],
        (who, x_other, w_enc, acc, b_enc.reshape(1, LOCAL), w_dec),
        [SM, VM, VM, VM, VM, VM],
        flops=4 * ROWS * HALF * LOCAL,
        nbytes=12 * MIB,
    )
    part_recv = swap(part_send)
    part_own, norm_rows, norm_cols = call(
        decode_own_kernel,
        [((ROWS, HALF), f32), ((2, LOCAL), f32), ((LOCAL, 2), f32)],
        (who, feats, w_dec),
        [SM, VM, VM],
        flops=2 * ROWS * HALF * LOCAL,
        nbytes=10 * MIB,
    )
    (part,) = call(add_kernel, [((ROWS, HALF), bf16)], (part_own, part_recv))
    parts = lax.all_to_all(part.reshape(CHIPS, 8, HALF), ("x", "y"), split_axis=0, concat_axis=0, tiled=True)
    (block,) = call(
        err_kernel,
        [((CHIPS, 8, HALF + PAD), bf16)],
        (who, parts, mine, b_dec, feats, norm_rows),
        [SM] + [VM] * 5,
    )
    e_own = lax.all_to_all(block, ("x", "y"), split_axis=0, concat_axis=0, tiled=True).reshape(ROWS, HALF + PAD)
    e_other = swap(e_own)
    acc, *e_slices = call(
        dfeat_own_kernel,
        [((ROWS, LOCAL), f32)] + [((ROWS, SUB), bf16)] * NZ,
        (who, e_own, w_dec),
        [SM, VM, VM],
        flops=2 * ROWS * HALF * LOCAL,
        nbytes=6 * MIB,
    )
    (dpre,) = call(
        dpre_kernel,
        [((ROWS + 16, LOCAL), bf16)],
        (who, e_other, e_own, w_dec, acc, act, x_own, norm_rows),
        [SM] + [VM] * 7,
        flops=2 * ROWS * HALF * LOCAL,
        nbytes=6 * MIB,
    )

    def around(pieces):
        return [pieces[0]] + [shift(pieces[k], k) for k in range(1, NZ)]

    xs = around(x_slices)
    fs = around([feats] * NZ)
    es = around(e_slices)
    ds = around([dpre] * NZ)
    xs_other = [swap(v) for v in xs]
    es_other = [swap(v) for v in es]
    grad_enc, loss = call(
        grad_enc_kernel,
        [((2, SUB, LOCAL), bf16), ((1, 1), f32)],
        (who, *xs, *xs_other, *ds),
        [SM] + [VM] * 12,
        [pltpu.VMEM((NZ * ROWS, SUB), bf16), pltpu.VMEM((NZ * ROWS, LOCAL), bf16)],
        flops=2 * NZ * ROWS * 2 * SUB * LOCAL,
        nbytes=5 * MIB,
    )
    (grad_dec,) = call(
        grad_dec_kernel,
        [((LOCAL, 2 * SUB), bf16)],
        (who, *es, *es_other, *fs, *ds, norm_cols, w_dec),
        [SM] + [VM] * 18,
        [pltpu.VMEM((NZ * ROWS, SUB), bf16), pltpu.VMEM((NZ * ROWS, LOCAL), bf16)],
        flops=2 * NZ * ROWS * 2 * SUB * LOCAL,
        nbytes=7 * MIB,
    )
    return grad_enc, grad_dec, loss.reshape(())


def solution(mesh):
    fine = Mesh(mesh.devices.reshape(4, 4, 4, 2), ALL)
    lat = ("x", "y", "c")
    return jax.shard_map(
        shards,
        mesh=fine,
        in_specs=(P(ALL, None), P(ALL), P(ALL, None), P(None, None, lat), P(lat), P(lat, None), P()),
        out_specs=(P(None, "z", lat), P(lat, "z"), P()),
        check_vma=False,
    )
```

```python
import jax
import jax.numpy as jnp
from jax import lax
from jax.experimental import pallas as pl
from jax.experimental.pallas import tpu as pltpu
from jax.sharding import Mesh
from jax.sharding import PartitionSpec as P

sparsity_weight = 1.0
loss_scale = 8.0
norm_eps = 1e-06

ALL = ("z", "x", "y", "c")
NZ = 4
CHIPS = 16
WIDTH = 8192
HALF = 4096
SUB = 1024
LOCAL = 512
ROWS = 128
PAD = 128
MIB = 1 << 20
f32 = jnp.float32
bf16 = jnp.bfloat16

VM = pl.BlockSpec(memory_space=pltpu.VMEM)


def at_hbm(v):
    return pltpu.with_memory_space_constraint(v, pltpu.HBM)


def call(body, outs, args, specs=None, scratch=(), vmem=None, flops=0, nbytes=0, out_specs=None):
    return pl.pallas_call(
        body,
        out_shape=[pltpu.VMEM(o[0], o[1]) if len(o) == 3 else jax.ShapeDtypeStruct(*o) for o in outs],
        in_specs=specs or [VM] * len(args),
        out_specs=out_specs or [VM] * len(outs),
        scratch_shapes=list(scratch),
        compiler_params=pltpu.CompilerParams(vmem_limit_bytes=vmem or 16 * MIB),
        cost_estimate=pl.CostEstimate(flops=flops, bytes_accessed=nbytes, transcendentals=0),
    )(*args)


def lanes(start, size):
    return pl.ds(pl.multiple_of(start, 128), size)


def split3(v):
    hi = v.astype(bf16)
    rest = v - hi.astype(f32)
    mid = rest.astype(bf16)
    low = (rest - mid.astype(f32)).astype(bf16)
    return hi, mid, low


def prep_kernel(length, acts_hbm, group_hbm, keep, send, acts, group, sems):
    copies = [
        pltpu.make_async_copy(src, dst, sems.at[i])
        for i, (src, dst) in enumerate(((acts_hbm, acts), (group_hbm, group)))
    ]
    for copy in copies:
        copy.start()
    for copy in copies:
        copy.wait()
    c = lax.axis_index("c")
    slot = lax.broadcasted_iota(jnp.int32, (1, 5), 1)
    held = jnp.sum(jnp.where(group[...] == NZ, slot, 0), axis=1, keepdims=True)
    k = lax.broadcasted_iota(jnp.int32, (4, 1), 0)
    later = k >= held
    src = k + later.astype(jnp.int32)
    live = (src < length[0]).astype(f32)
    live = jnp.broadcast_to(live, (4, PAD)).astype(bf16)

    def pick(cols):
        rows = acts[:, cols].astype(f32)
        return jnp.where(later, rows[1:5], rows[0:4]).astype(bf16)

    for out, core in ((keep, c), (send, 1 - c)):
        out[:, :HALF] = pick(lanes(core * HALF, HALF))
        for q in range(NZ):
            out[:, HALF + q * SUB : HALF + (q + 1) * SUB] = pick(lanes(q * 2 * SUB + core * SUB, SUB))
        out[:, 2 * HALF :] = live


def join_kernel(own, other, out, mine):
    first = lax.axis_index("c") == 0
    a, b = own[...].astype(f32), other[...].astype(f32)
    rows = jnp.concatenate([jnp.where(first, a, b), jnp.where(first, b, a)], axis=0)
    mine[...] = rows[:, HALF:].astype(bf16)
    for i in range(CHIPS):
        out[i, :, :HALF] = rows[:, :HALF].astype(bf16)
        out[i, :, HALF:] = rows[:, 2 * HALF :].astype(bf16)


def norm_kernel(w_dec_hbm, norm_row, norm_col, w_dec, sems):
    rows = LOCAL // 4
    copies = [
        pltpu.make_async_copy(w_dec_hbm.at[pl.ds(i * rows, rows)], w_dec.at[pl.ds(i * rows, rows)], sems.at[i])
        for i in range(4)
    ]
    for copy in copies:
        copy.start()
    for i in range(4):
        copies[i].wait()
        n = i * rows
        for s in range(2):

            def add(j, total):
                for m in range(4):
                    v = w_dec[n : n + rows, lanes(s * HALF + j * 512 + m * 128, 128)].astype(f32)
                    total = total + v * v
                return total

            total = lax.fori_loop(0, HALF // 512, add, jnp.zeros((rows, 128), f32))
            norm_row[s : s + 1, n : n + rows] = jnp.sqrt(jnp.sum(total.T, axis=0, keepdims=True) + norm_eps)
            norm_col[n : n + rows, s : s + 1] = jnp.sqrt(jnp.sum(total, axis=1, keepdims=True) + norm_eps)


def fetch_enc(w_hbm, core, buf, sems, at=0):
    copies = [
        pltpu.make_async_copy(w_hbm.at[core, pl.ds(i * SUB, SUB)], buf.at[i], sems.at[at + i]) for i in range(4)
    ]
    for copy in copies:
        copy.start()
    return copies


def fetch_dec(w_hbm, core, buf, sems, at=0):
    copies = [
        pltpu.make_async_copy(w_hbm.at[:, lanes(q * 2 * SUB + core * SUB, SUB)], buf.at[q], sems.at[at + q])
        for q in range(NZ)
    ]
    for copy in copies:
        copy.start()
    return copies


def project(x, copies, buf, acc):
    for i in range(4):
        if copies:
            copies[i].wait()
        for n in range(0, LOCAL, 256):
            acc[:, n : n + 256] += jnp.dot(
                x[:, i * SUB : (i + 1) * SUB], buf[i, :, n : n + 256], preferred_element_type=f32
            )


def encode_own_kernel(x, w_enc, acc, rest, mask, buf, sems):
    c = lax.axis_index("c")
    copies = fetch_enc(w_enc, c, buf, sems)
    later = fetch_enc(w_enc, 1 - c, rest, sems, 4)
    acc[...] = jnp.zeros_like(acc)
    mask[...] = x[:, HALF:]
    project(x, copies, buf, acc)
    for copy in later:
        copy.wait()


def encode_kernel(x, mask, part, bias, w_enc, w_dec, act_out, feats_out, send, acc, dec, dec_sems):
    c = lax.axis_index("c")
    dec_copies = fetch_dec(w_dec, 1 - c, dec, dec_sems)
    live = mask[:, 0:1].astype(f32)
    count = jnp.sum(live, axis=0, keepdims=True)
    acc[...] = part[...]
    project(x, None, w_enc, acc)
    for n in range(0, LOCAL, 256):
        act = jnp.maximum(acc[:, n : n + 256] + bias[:, n : n + 256], 0.0)
        feats = act * act
        act_out[:, n : n + 256] = act
        feats_out[:ROWS, n : n + 256] = feats.astype(bf16)
        fsum = jnp.sum(feats * live, axis=0, keepdims=True)
        tail = jnp.zeros((16, 256), f32)
        row = lax.broadcasted_iota(jnp.int32, (16, 256), 0)
        for i, piece in enumerate((*split3(fsum), jnp.broadcast_to(count, (1, 256)))):
            tail = jnp.where(row == i, piece.astype(f32), tail)
        feats_out[ROWS:, n : n + 256] = tail.astype(bf16)
    feats16 = feats_out[:ROWS, :]
    for q in range(NZ):
        dec_copies[q].wait()
        send[:, q * SUB : (q + 1) * SUB] = jnp.dot(feats16, dec[q], preferred_element_type=f32).astype(bf16)


def decode_own_kernel(feats, w_dec, part, buf, sems):
    copies = fetch_dec(w_dec, lax.axis_index("c"), buf, sems)
    feats16 = feats[:ROWS, :]
    for q in range(NZ):
        copies[q].wait()
        part[:, q * SUB : (q + 1) * SUB] = jnp.dot(feats16, buf[q], preferred_element_type=f32)


def pack_kernel(x, *pieces):
    z = lax.axis_index("z")
    for k in range(1, NZ):
        pieces[k - 1][...] = x[:, lanes(lax.rem(z + k, NZ) * SUB, SUB)]


def add_kernel(own, other, out):
    for n in range(0, HALF, SUB):
        out[:, n : n + SUB] = (own[:, n : n + SUB] + other[:, n : n + SUB].astype(f32)).astype(bf16)


def err_kernel(parts, mine, bias, feats, norm_row, out):
    c = lax.axis_index("c")
    live = mine[:, HALF : HALF + 1].astype(f32)
    square = jnp.zeros((8, SUB), f32)
    for q in range(NZ):
        cols = slice(q * SUB, (q + 1) * SUB)
        total = parts[0, :, cols].astype(f32)
        for i in range(1, CHIPS):
            total = total + parts[i, :, cols].astype(f32)
        add = bias[q // 2 : q // 2 + 1, lanes((q % 2) * 2 * SUB + c * SUB, SUB)]
        err = (total + add - mine[:, cols].astype(f32)) * live
        square = square + err * err
        err16 = err.astype(bf16)
        for i in range(CHIPS):
            out[i, :, cols] = err16
    squares = jnp.sum(jnp.sum(square, axis=0, keepdims=True), axis=1, keepdims=True)
    fsum = jnp.sum(feats[ROWS : ROWS + 3, :].astype(f32), axis=0, keepdims=True)
    nsum = norm_row[0:1, :] + norm_row[1:2, :]
    sparse = sparsity_weight * jnp.sum(fsum * nsum, axis=1, keepdims=True)
    lane = lax.broadcasted_iota(jnp.int32, (8, PAD), 1)
    row = lax.broadcasted_iota(jnp.int32, (8, PAD), 0)
    tail = jnp.zeros((8, PAD), f32)
    for i, piece in enumerate(split3(squares + sparse)):
        tail = jnp.where((lane == i) & (row == 0), piece.astype(f32), tail)
    for i in range(CHIPS):
        out[i, :, HALF:] = tail.astype(bf16)


def dfeat(e, copies, buf, acc):
    for q in range(NZ):
        if copies:
            copies[q].wait()
        for n in range(0, LOCAL, 256):
            acc[:, n : n + 256] += lax.dot_general(
                e[:, q * SUB : (q + 1) * SUB],
                buf[q, n : n + 256, :],
                (((1,), (1,)), ((), ())),
                preferred_element_type=f32,
            )


def dfeat_own_kernel(e, w_dec, acc, rest, s1, s2, s3, buf, sems):
    z, c = lax.axis_index("z"), lax.axis_index("c")
    copies = fetch_dec(w_dec, c, buf, sems)
    later = fetch_dec(w_dec, 1 - c, rest, sems, 4)
    for k, out in enumerate((s1, s2, s3)):
        out[...] = e[:, lanes(lax.rem(z + k + 1, NZ) * SUB, SUB)]
    acc[...] = jnp.zeros_like(acc)
    dfeat(e, copies, buf, acc)
    for copy in later:
        copy.wait()


def dpre_kernel(e, own, part, act, mask, norm_row, w_dec, out, acc):
    acc[...] = part[...]
    both = e[:, HALF:].astype(f32) + own[:, HALF:].astype(f32)
    both = jnp.sum(jnp.sum(both, axis=0, keepdims=True), axis=1, keepdims=True)
    lane = lax.broadcasted_iota(jnp.int32, (16, LOCAL), 1)
    tail = jnp.zeros((16, LOCAL), f32)
    for i, piece in enumerate(split3(both)):
        tail = jnp.where(lane == i, piece.astype(f32), tail)
    out[ROWS:, :] = tail.astype(bf16)
    live = mask[:, 0:1].astype(f32)
    dfeat(e, None, w_dec, acc)
    for n in range(0, LOCAL, 256):
        nsum = norm_row[0:1, n : n + 256] + norm_row[1:2, n : n + 256]
        grad = 2.0 * acc[:, n : n + 256] + sparsity_weight * live * nsum
        out[:ROWS, n : n + 256] = (grad * 2.0 * act[:, n : n + 256]).astype(bf16)


def merge_kernel(a, b, d, *refs):
    out = refs[-1]
    for k, v in enumerate((a, b, d)):
        out[k * ROWS : (k + 1) * ROWS, :] = v[...]


def count_of(feats):
    count = jnp.zeros((1, 1), f32)
    for p in feats:
        count = count + p[ROWS + 3 : ROWS + 4, 0:1].astype(f32)
    return count


def grad_enc_kernel(*refs):
    z, c = lax.axis_index("z"), lax.axis_index("c")
    x_own, x_other, own, other, feats, pres = *refs[0:4], refs[4:8], refs[8:12]
    out, loss, xs, ds, done, sems = refs[12:]
    count = count_of(feats)
    total = jnp.zeros((1, 1), f32)
    for k in range(NZ):
        total = total + jnp.sum(pres[k][ROWS : ROWS + 1, 0:3].astype(f32), axis=1, keepdims=True)
        ds[k * ROWS : (k + 1) * ROWS, :] = pres[k][:ROWS, :]
    loss[...] = total / (count * WIDTH)
    factor = loss_scale / count
    copies = []
    for side, plane, rest in ((c, x_own, own), (1 - c, x_other, other)):
        xs[:ROWS, :] = plane[:, lanes(z * SUB, SUB)]
        xs[ROWS:, :] = rest[...]
        for n in range(0, SUB, 256):
            part = lax.dot_general(
                xs[:, n : n + 256], ds[...], (((0,), (0,)), ((), ())), preferred_element_type=f32
            )
            done[side, n : n + 256, :] = (part * factor).astype(bf16)
            piece = pl.ds(n, 256)
            copies.append(pltpu.make_async_copy(done.at[side, piece], out.at[side, piece], sems.at[len(copies)]))
            copies[-1].start()
    for copy in copies:
        copy.wait()


def grad_dec_kernel(*refs):
    z, c = lax.axis_index("z"), lax.axis_index("c")
    e_own, e_other, own, other, feats, norm_col, w_dec = *refs[0:4], refs[4:8], refs[8], refs[9]
    out, es, fs, done, w, w_sem, sems = refs[10:]
    fetch = pltpu.make_async_copy(w_dec.at[:, lanes(z * 2 * SUB, 2 * SUB)], w, w_sem)
    fetch.start()
    factor = loss_scale / count_of(feats)
    fsum = jnp.zeros((1, LOCAL), f32)
    for k in range(NZ):
        fs[k * ROWS : (k + 1) * ROWS, :] = feats[k][:ROWS, :]
        fsum = fsum + jnp.sum(feats[k][ROWS : ROWS + 3, :].astype(f32), axis=0, keepdims=True)
    fsum = jnp.broadcast_to(fsum, (128, LOCAL)).T[:, 0:1]
    norm = jnp.where(z < 2, norm_col[:, 0:1], norm_col[:, 1:2])
    scale = sparsity_weight * fsum / norm
    for side, plane, rest in ((c, e_own, own), (1 - c, e_other, other)):
        es[:ROWS, lanes(side * SUB, SUB)] = plane[:, lanes(z * SUB, SUB)]
        es[ROWS:, lanes(side * SUB, SUB)] = rest[...]
    copies = []
    for n in range(0, LOCAL, 256):
        piece = pl.ds(n, 256)
        for m in range(0, 2 * SUB, 512):
            part = 2.0 * lax.dot_general(
                fs[:, n : n + 256], es[:, m : m + 512], (((0,), (0,)), ((), ())), preferred_element_type=f32
            )
            if n == m == 0:
                fetch.wait()
            part = part + scale[n : n + 256, :] * w[n : n + 256, m : m + 512].astype(f32)
            done[n : n + 256, m : m + 512] = (part * factor).astype(bf16)
        copies.append(pltpu.make_async_copy(done.at[piece], out.at[piece], sems.at[len(copies)]))
        copies[-1].start()
    for copy in copies:
        copy.wait()


def swap(v):
    return lax.ppermute(v, "c", [(0, 1), (1, 0)])


def chips(v):
    return lax.all_to_all(v, ("x", "y"), split_axis=0, concat_axis=0, tiled=True)


def planes(v):
    return lax.all_to_all(v, "z", split_axis=0, concat_axis=0, tiled=True)


def shift(v, k):
    return lax.ppermute(v, "z", [(i, (i + k) % NZ) for i in range(NZ)])


def shards(acts, chat_len, group_of, w_enc, b_enc, w_dec, b_dec):
    half_flops = 2 * ROWS * HALF * LOCAL
    w_enc, w_dec = at_hbm(w_enc), at_hbm(w_dec)
    hbm = pl.BlockSpec(memory_space=pltpu.HBM)
    enc_scratch = [pltpu.VMEM((4, SUB, LOCAL), bf16), pltpu.SemaphoreType.DMA((4,))]
    dec_scratch = [pltpu.VMEM((4, LOCAL, SUB), bf16), pltpu.SemaphoreType.DMA((4,))]
    acc_scratch = pltpu.VMEM((ROWS, LOCAL), f32)
    keep, send = call(
        prep_kernel,
        [((4, 2 * HALF + PAD), bf16)] * 2,
        (chat_len, at_hbm(acts), at_hbm(group_of.reshape(1, 5))),
        [pl.BlockSpec(memory_space=pltpu.SMEM), hbm, hbm],
        [
            pltpu.VMEM((5, WIDTH), bf16),
            pltpu.VMEM((1, 5), jnp.int32),
            pltpu.SemaphoreType.DMA((2,)),
        ],
    )
    block, mine = call(
        join_kernel,
        [((CHIPS, 8, HALF + PAD), bf16), ((8, HALF + PAD), bf16)],
        (keep, swap(send)),
    )
    norm_row, norm_col = call(
        norm_kernel,
        [((2, LOCAL), f32), ((LOCAL, 2), f32)],
        (w_dec,),
        [hbm],
        [pltpu.VMEM((LOCAL, WIDTH), bf16), pltpu.SemaphoreType.DMA((4,))],
        flops=4 * LOCAL * WIDTH,
        nbytes=8 * MIB,
    )
    x_own, norm_row, norm_col = lax.optimization_barrier((chips(block), norm_row, norm_col))
    x_own = x_own.reshape(ROWS, HALF + PAD)
    x_other = swap(x_own)
    acc, w_rest, mask = call(
        encode_own_kernel,
        [((ROWS, LOCAL), f32), ((4, SUB, LOCAL), bf16, 1), ((ROWS, PAD), bf16)],
        (x_own, w_enc),
        [VM, hbm],
        [enc_scratch[0], pltpu.SemaphoreType.DMA((8,))],
        flops=half_flops,
        nbytes=10 * MIB,
    )
    act, feats, part_send = call(
        encode_kernel,
        [((ROWS, LOCAL), f32), ((ROWS + 16, LOCAL), bf16), ((ROWS, HALF), bf16)],
        (x_other, mask, acc, b_enc.reshape(1, LOCAL), w_rest, w_dec),
        [VM] * 5 + [hbm],
        [acc_scratch, *dec_scratch],
        flops=2 * half_flops,
        nbytes=8 * MIB,
    )
    part_recv = swap(part_send)
    (part_own,) = call(
        decode_own_kernel,
        [((ROWS, HALF), f32)],
        (feats, w_dec),
        [VM, hbm],
        dec_scratch,
        flops=half_flops,
        nbytes=6 * MIB,
    )
    (part,) = call(add_kernel, [((ROWS, HALF), bf16)], (part_own, part_recv))
    parts = chips(part.reshape(CHIPS, 8, HALF))
    xs = call(pack_kernel, [((ROWS, SUB), bf16)] * 3, (x_own,), nbytes=2 * MIB)
    xs = [shift(xs[k - 1], k) for k in range(1, NZ)]
    parts, *xs = lax.optimization_barrier((parts, *xs))
    (block,) = call(
        err_kernel,
        [((CHIPS, 8, HALF + PAD), bf16)],
        (parts, mine, b_dec, feats, norm_row),
    )
    fs = [feats] + [shift(feats, k) for k in range(1, NZ)]
    e_own, *fs = lax.optimization_barrier((chips(block), *fs))
    e_own = e_own.reshape(ROWS, HALF + PAD)
    e_other = swap(e_own)
    acc, w_rest, *slices = call(
        dfeat_own_kernel,
        [((ROWS, LOCAL), f32), ((4, LOCAL, SUB), bf16, 1)] + [((ROWS, SUB), bf16)] * 3,
        (e_own, w_dec),
        [VM, hbm],
        [dec_scratch[0], pltpu.SemaphoreType.DMA((8,))],
        flops=half_flops,
        nbytes=10 * MIB,
    )
    es = [shift(slices[k - 1], k) for k in range(1, NZ)]
    (dpre,) = call(
        dpre_kernel,
        [((ROWS + 16, LOCAL), bf16)],
        (e_other, e_own, acc, act, mask, norm_row, w_rest),
        scratch=[acc_scratch],
        flops=half_flops,
        nbytes=2 * MIB,
    )
    ds = [dpre] + [shift(dpre, k) for k in range(1, NZ)]
    anywhere = pl.BlockSpec(memory_space=pl.ANY)
    (xs,) = call(merge_kernel, [((3 * ROWS, SUB), bf16)], (*xs, dpre), [VM] * 3 + [anywhere], nbytes=2 * MIB)
    (es,) = call(merge_kernel, [((3 * ROWS, SUB), bf16)], (*es, *ds[1:]), [VM] * 3 + [anywhere] * 3, nbytes=2 * MIB)
    grad_enc, loss = call(
        grad_enc_kernel,
        [((2, SUB, LOCAL), bf16), ((1, 1), f32)],
        (x_own, x_other, xs, swap(xs), *fs, *ds),
        scratch=[
            pltpu.VMEM((NZ * ROWS, SUB), bf16),
            pltpu.VMEM((NZ * ROWS, LOCAL), bf16),
            pltpu.VMEM((2, SUB, LOCAL), bf16),
            pltpu.SemaphoreType.DMA((8,)),
        ],
        out_specs=[hbm, VM],
        flops=4 * half_flops,
        nbytes=5 * MIB,
    )
    (grad_dec,) = call(
        grad_dec_kernel,
        [((LOCAL, 2 * SUB), bf16)],
        (e_own, e_other, es, swap(es), *fs, norm_col, w_dec),
        [VM] * 9 + [hbm],
        [
            pltpu.VMEM((NZ * ROWS, 2 * SUB), bf16),
            pltpu.VMEM((NZ * ROWS, LOCAL), bf16),
            pltpu.VMEM((LOCAL, 2 * SUB), bf16),
            pltpu.VMEM((LOCAL, 2 * SUB), bf16),
            pltpu.SemaphoreType.DMA,
            pltpu.SemaphoreType.DMA((2,)),
        ],
        out_specs=[hbm],
        flops=4 * half_flops,
        nbytes=7 * MIB,
    )
    return grad_enc, grad_dec, loss.reshape(())


def solution(mesh):
    fine = Mesh(mesh.devices.reshape(4, 4, 4, 2), ALL)
    lat = ("x", "y", "c")
    return jax.shard_map(
        shards,
        mesh=fine,
        in_specs=(P(ALL, None), P(ALL), P(ALL, None), P(None, None, lat), P(lat), P(lat, None), P()),
        out_specs=(P(None, "z", lat), P(lat, "z"), P()),
        check_vma=False,
    )
```

```python
import jax
import jax.numpy as jnp
from jax import lax
from jax.experimental import pallas as pl
from jax.experimental.pallas import tpu as pltpu
from jax.sharding import Mesh
from jax.sharding import PartitionSpec as P

sparsity_weight = 1.0
loss_scale = 8.0
norm_eps = 1e-06

ALL = ("z", "x", "y", "c")
NZ = 4
CHIPS = 16
WIDTH = 8192
HALF = 4096
SUB = 1024
LOCAL = 512
ROWS = 128
PAD = 128
MIB = 1 << 20
f32 = jnp.float32
bf16 = jnp.bfloat16

VM = pl.BlockSpec(memory_space=pltpu.VMEM)


def at_hbm(v):
    return pltpu.with_memory_space_constraint(v, pltpu.HBM)


def call(body, outs, args, specs=None, scratch=(), vmem=None, flops=0, nbytes=0, out_specs=None):
    return pl.pallas_call(
        body,
        out_shape=[o[2](o[0], o[1]) if len(o) == 3 else jax.ShapeDtypeStruct(*o) for o in outs],
        in_specs=specs or [VM] * len(args),
        out_specs=out_specs or [VM] * len(outs),
        scratch_shapes=list(scratch),
        compiler_params=pltpu.CompilerParams(vmem_limit_bytes=vmem or 16 * MIB),
        cost_estimate=pl.CostEstimate(flops=flops, bytes_accessed=nbytes, transcendentals=0),
    )(*args)


def lanes(start, size):
    return pl.ds(pl.multiple_of(start, 128), size)


def split3(v):
    hi = v.astype(bf16)
    rest = v - hi.astype(f32)
    mid = rest.astype(bf16)
    low = (rest - mid.astype(f32)).astype(bf16)
    return hi, mid, low


def prep_kernel(length, acts_hbm, group_hbm, keep, send, acts, group, sems):
    copies = [
        pltpu.make_async_copy(src, dst, sems.at[i])
        for i, (src, dst) in enumerate(((acts_hbm, acts), (group_hbm, group)))
    ]
    for copy in copies:
        copy.start()
    for copy in copies:
        copy.wait()
    c = lax.axis_index("c")
    slot = lax.broadcasted_iota(jnp.int32, (1, 5), 1)
    held = jnp.sum(jnp.where(group[...] == NZ, slot, 0), axis=1, keepdims=True)
    k = lax.broadcasted_iota(jnp.int32, (4, 1), 0)
    later = k >= held
    src = k + later.astype(jnp.int32)
    live = (src < length[0]).astype(f32)
    live = jnp.broadcast_to(live, (4, PAD)).astype(bf16)

    def pick(cols):
        rows = acts[:, cols].astype(f32)
        return jnp.where(later, rows[1:5], rows[0:4]).astype(bf16)

    for out, core in ((keep, c), (send, 1 - c)):
        out[:, :HALF] = pick(lanes(core * HALF, HALF))
        for q in range(NZ):
            out[:, HALF + q * SUB : HALF + (q + 1) * SUB] = pick(lanes(q * 2 * SUB + core * SUB, SUB))
        out[:, 2 * HALF :] = live


def join_kernel(own, other, out, mine):
    first = lax.axis_index("c") == 0
    a, b = own[...].astype(f32), other[...].astype(f32)
    rows = jnp.concatenate([jnp.where(first, a, b), jnp.where(first, b, a)], axis=0)
    mine[...] = rows[:, HALF:].astype(bf16)
    for i in range(CHIPS):
        out[i, :, :HALF] = rows[:, :HALF].astype(bf16)
        out[i, :, HALF:] = rows[:, 2 * HALF :].astype(bf16)


def norm_kernel(w_dec_hbm, norm_row, norm_col, w_dec, sems):
    rows = LOCAL // 4
    copies = [
        pltpu.make_async_copy(w_dec_hbm.at[pl.ds(i * rows, rows)], w_dec.at[pl.ds(i * rows, rows)], sems.at[i])
        for i in range(4)
    ]
    for copy in copies:
        copy.start()
    for i in range(4):
        copies[i].wait()
        n = i * rows
        for s in range(2):

            def add(j, total):
                for m in range(4):
                    v = w_dec[n : n + rows, lanes(s * HALF + j * 512 + m * 128, 128)].astype(f32)
                    total = total + v * v
                return total

            total = lax.fori_loop(0, HALF // 512, add, jnp.zeros((rows, 128), f32))
            norm_row[s : s + 1, n : n + rows] = jnp.sqrt(jnp.sum(total.T, axis=0, keepdims=True) + norm_eps)
            norm_col[n : n + rows, s : s + 1] = jnp.sqrt(jnp.sum(total, axis=1, keepdims=True) + norm_eps)


def fetch_enc(w_hbm, core, buf, sems, at=0):
    copies = [
        pltpu.make_async_copy(w_hbm.at[core, pl.ds(i * SUB, SUB)], buf.at[pl.ds(i * SUB, SUB)], sems.at[at + i])
        for i in range(4)
    ]
    for copy in copies:
        copy.start()
    return copies


def fetch_dec(w_hbm, core, buf, sems, at=0):
    copies = [
        pltpu.make_async_copy(w_hbm.at[:, lanes(q * 2 * SUB + core * SUB, SUB)], buf.at[q], sems.at[at + q])
        for q in range(NZ)
    ]
    for copy in copies:
        copy.start()
    return copies


def encode_own_kernel(x, w_enc, acc, rest, mask, home, p1, p2, p3, buf, sems):
    z, c = lax.axis_index("z"), lax.axis_index("c")
    copies = fetch_enc(w_enc, c, buf, sems)
    later = fetch_enc(w_enc, 1 - c, rest, sems, 4)
    mask[...] = x[:, HALF:]
    home[...] = x[:, lanes(z * SUB, SUB)]
    for k, out in enumerate((p1, p2, p3)):
        out[...] = x[:, lanes(lax.rem(z + k + 1, NZ) * SUB, SUB)]
    for i in range(0, 4, 2):
        copies[i].wait()
        copies[i + 1].wait()
        rows = slice(i * SUB, (i + 2) * SUB)
        for n in range(0, LOCAL, 256):
            part = jnp.dot(x[:, rows], buf[rows, n : n + 256], preferred_element_type=f32)
            acc[:, n : n + 256] = part if i == 0 else acc[:, n : n + 256] + part
    for copy in later:
        copy.wait()


def encode_kernel(x, mask, part, bias, w_enc, w_dec, act_out, feats_out, send, home, dec, dec_sems):
    z, c = lax.axis_index("z"), lax.axis_index("c")
    dec_copies = fetch_dec(w_dec, 1 - c, dec, dec_sems)
    home[...] = x[:, lanes(z * SUB, SUB)]
    live = mask[:, 0:1].astype(f32)
    count = jnp.sum(live, axis=0, keepdims=True)
    for n in range(0, LOCAL, 256):
        pre = part[:, n : n + 256] + jnp.dot(x[:, :HALF], w_enc[:, n : n + 256], preferred_element_type=f32)
        act = jnp.maximum(pre + bias[:, n : n + 256], 0.0)
        feats = act * act
        act_out[:, n : n + 256] = act
        feats_out[:ROWS, n : n + 256] = feats.astype(bf16)
        fsum = jnp.sum(feats * live, axis=0, keepdims=True)
        tail = jnp.zeros((16, 256), f32)
        row = lax.broadcasted_iota(jnp.int32, (16, 256), 0)
        for i, piece in enumerate((*split3(fsum), jnp.broadcast_to(count, (1, 256)))):
            tail = jnp.where(row == i, piece.astype(f32), tail)
        feats_out[ROWS:, n : n + 256] = tail.astype(bf16)
    feats16 = feats_out[:ROWS, :]
    for q in range(NZ):
        dec_copies[q].wait()
        send[:, q * SUB : (q + 1) * SUB] = jnp.dot(feats16, dec[q], preferred_element_type=f32).astype(bf16)


def decode_own_kernel(feats, w_dec, part, buf, sems):
    copies = fetch_dec(w_dec, lax.axis_index("c"), buf, sems)
    feats16 = feats[:ROWS, :]
    for q in range(NZ):
        copies[q].wait()
        part[:, q * SUB : (q + 1) * SUB] = jnp.dot(feats16, buf[q], preferred_element_type=f32)


def turn_kernel(home_own, home_other, own, other, *refs):
    z, c = lax.axis_index("z"), lax.axis_index("c")
    feats, norm_col, w_dec = refs[0:4], refs[4], refs[5]
    xt, ft, scale, count, w, sem = refs[7:]
    fetch = pltpu.make_async_copy(w_dec.at[:, lanes(z * 2 * SUB, 2 * SUB)], w, sem)
    fetch.start()
    fsum = jnp.zeros((1, LOCAL), f32)
    total = jnp.zeros((1, 1), f32)
    for side, mine, rest in ((c, home_own, own), (1 - c, home_other, other)):
        xt[side, :, :ROWS] = mine[...].T
        for k in range(1, NZ):
            xt[side, :, k * ROWS : (k + 1) * ROWS] = rest[(k - 1) * ROWS : k * ROWS, :].T
    for k in range(NZ):
        ft[:, k * ROWS : (k + 1) * ROWS] = feats[k][:ROWS, :].T
        fsum = fsum + jnp.sum(feats[k][ROWS : ROWS + 3, :].astype(f32), axis=0, keepdims=True)
        total = total + feats[k][ROWS + 3 : ROWS + 4, 0:1].astype(f32)
    count[...] = total
    fsum = jnp.broadcast_to(fsum, (128, LOCAL)).T[:, 0:1]
    norm = jnp.where(z < 2, norm_col[:, 0:1], norm_col[:, 1:2])
    scale[...] = sparsity_weight * fsum / norm
    fetch.wait()


def add_kernel(own, other, out):
    for n in range(0, HALF, SUB):
        out[:, n : n + SUB] = (own[:, n : n + SUB] + other[:, n : n + SUB].astype(f32)).astype(bf16)


def err_kernel(parts, mine, bias, feats, norm_row, out):
    c = lax.axis_index("c")
    live = mine[:, HALF : HALF + 1].astype(f32)
    square = jnp.zeros((8, SUB), f32)
    for q in range(NZ):
        cols = slice(q * SUB, (q + 1) * SUB)
        total = parts[0, :, cols].astype(f32)
        for i in range(1, CHIPS):
            total = total + parts[i, :, cols].astype(f32)
        add = bias[q // 2 : q // 2 + 1, lanes((q % 2) * 2 * SUB + c * SUB, SUB)]
        err = (total + add - mine[:, cols].astype(f32)) * live
        square = square + err * err
        err16 = err.astype(bf16)
        for i in range(CHIPS):
            out[i, :, cols] = err16
    squares = jnp.sum(jnp.sum(square, axis=0, keepdims=True), axis=1, keepdims=True)
    fsum = jnp.sum(feats[ROWS : ROWS + 3, :].astype(f32), axis=0, keepdims=True)
    nsum = norm_row[0:1, :] + norm_row[1:2, :]
    sparse = sparsity_weight * jnp.sum(fsum * nsum, axis=1, keepdims=True)
    lane = lax.broadcasted_iota(jnp.int32, (8, PAD), 1)
    row = lax.broadcasted_iota(jnp.int32, (8, PAD), 0)
    tail = jnp.zeros((8, PAD), f32)
    for i, piece in enumerate(split3(squares + sparse)):
        tail = jnp.where((lane == i) & (row == 0), piece.astype(f32), tail)
    for i in range(CHIPS):
        out[i, :, HALF:] = tail.astype(bf16)


def slice_kernel(e, s1, s2, s3):
    z = lax.axis_index("z")
    for k, out in enumerate((s1, s2, s3)):
        out[...] = e[:, lanes(lax.rem(z + k + 1, NZ) * SUB, SUB)]


def dpre_kernel(own, e, mask, norm_row, act_hbm, w_dec, out, act, buf, act_sem, sems):
    c = lax.axis_index("c")
    copies = fetch_dec(w_dec, c, buf.at[0], sems) + fetch_dec(w_dec, 1 - c, buf.at[1], sems, 4)
    fetch = pltpu.make_async_copy(act_hbm, act, act_sem)
    fetch.start()
    both = e[:, HALF:].astype(f32) + own[:, HALF:].astype(f32)
    both = jnp.sum(jnp.sum(both, axis=0, keepdims=True), axis=1, keepdims=True)
    lane = lax.broadcasted_iota(jnp.int32, (16, LOCAL), 1)
    tail = jnp.zeros((16, LOCAL), f32)
    for i, piece in enumerate(split3(both)):
        tail = jnp.where(lane == i, piece.astype(f32), tail)
    out[ROWS:, :] = tail.astype(bf16)
    live = mask[:, 0:1].astype(f32)
    totals = [jnp.zeros((ROWS, 256), f32), jnp.zeros((ROWS, 256), f32)]
    for q in range(2 * NZ):
        copies[q].wait()
        rows = (own, e)[q // NZ]
        for i in range(2):
            totals[i] = totals[i] + lax.dot_general(
                rows[:, (q % NZ) * SUB : (q % NZ + 1) * SUB],
                buf[q // NZ, q % NZ, i * 256 : (i + 1) * 256, :],
                (((1,), (1,)), ((), ())),
                preferred_element_type=f32,
            )
    fetch.wait()
    for i in range(2):
        n = slice(i * 256, (i + 1) * 256)
        nsum = norm_row[0:1, n] + norm_row[1:2, n]
        grad = 2.0 * totals[i] + sparsity_weight * live * nsum
        out[:ROWS, n] = (grad * 2.0 * act[:, n]).astype(bf16)


def merge_kernel(a, b, d, out):
    for k, v in enumerate((a, b, d)):
        out[k * ROWS : (k + 1) * ROWS, :] = v[...]


def part_kernel(*refs):
    pres, slices, count = refs[0:4], refs[4:7], refs[7]
    es, ds, loss = refs[8:]
    total = jnp.zeros((1, 1), f32)
    for k, p in enumerate(pres):
        total = total + jnp.sum(p[ROWS : ROWS + 1, 0:3].astype(f32), axis=1, keepdims=True)
        ds[k * ROWS : (k + 1) * ROWS, :] = p[:ROWS, :]
    for k, p in enumerate(slices):
        es[k * ROWS : (k + 1) * ROWS, :] = p[...]
    loss[...] = total / (count[...] * WIDTH)


def grad_enc_kernel(xt, count, ds, out, done, sems):
    factor = loss_scale / count[...]
    copies = []
    for i in range(4):
        rows = pl.ds(i % 2 * 512, 512)
        for n in range(0, 512, 256):
            at = i % 2 * 512 + n
            part = jnp.dot(xt[i // 2, at : at + 256, :], ds[...], preferred_element_type=f32)
            done[i // 2, at : at + 256, :] = (part * factor).astype(bf16)
        copies.append(pltpu.make_async_copy(done.at[i // 2, rows], out.at[i // 2, rows], sems.at[i]))
        copies[-1].start()
    for copy in copies:
        copy.wait()


def grad_dec_kernel(e_own, e_other, own, other, ft, scale, count, w, out, es, done, sems):
    z, c = lax.axis_index("z"), lax.axis_index("c")
    factor = loss_scale / count[...]
    for side, plane, rest in ((c, e_own, own), (1 - c, e_other, other)):
        es[:ROWS, lanes(side * SUB, SUB)] = plane[:, lanes(z * SUB, SUB)]
        es[ROWS:, lanes(side * SUB, SUB)] = rest[...]
    copies = []
    for i, n in enumerate(range(0, LOCAL, 128)):
        for m in range(0, 2 * SUB, 512):
            part = 2.0 * jnp.dot(ft[n : n + 128, :], es[:, m : m + 512], preferred_element_type=f32)
            part = part + scale[n : n + 128, :] * w[n : n + 128, m : m + 512].astype(f32)
            done[n : n + 128, m : m + 512] = (part * factor).astype(bf16)
        piece = pl.ds(n, 128)
        copies.append(pltpu.make_async_copy(done.at[piece], out.at[piece], sems.at[i]))
        copies[-1].start()
    for copy in copies:
        copy.wait()


def swap(v):
    return lax.ppermute(v, "c", [(0, 1), (1, 0)])


def chips(v):
    return lax.all_to_all(v, ("x", "y"), split_axis=0, concat_axis=0, tiled=True)


def planes(v):
    return lax.all_to_all(v, "z", split_axis=0, concat_axis=0, tiled=True)


def shift(v, k):
    return lax.ppermute(v, "z", [(i, (i + k) % NZ) for i in range(NZ)])


def shards(acts, chat_len, group_of, w_enc, b_enc, w_dec, b_dec):
    half_flops = 2 * ROWS * HALF * LOCAL
    w_enc, w_dec = at_hbm(w_enc), at_hbm(w_dec)
    dec_scratch = [pltpu.VMEM((4, LOCAL, SUB), bf16), pltpu.SemaphoreType.DMA((4,))]
    hbm = pl.BlockSpec(memory_space=pltpu.HBM)
    anywhere = pl.BlockSpec(memory_space=pl.ANY)
    keep, send = call(
        prep_kernel,
        [((4, 2 * HALF + PAD), bf16)] * 2,
        (chat_len, at_hbm(acts), at_hbm(group_of.reshape(1, 5))),
        [pl.BlockSpec(memory_space=pltpu.SMEM), hbm, hbm],
        [
            pltpu.VMEM((5, WIDTH), bf16),
            pltpu.VMEM((1, 5), jnp.int32),
            pltpu.SemaphoreType.DMA((2,)),
        ],
        vmem=4 * MIB,
    )
    block, mine = call(
        join_kernel,
        [((CHIPS, 8, HALF + PAD), bf16), ((8, HALF + PAD), bf16)],
        (keep, swap(send)),
        vmem=4 * MIB,
    )
    norm_row, norm_col = call(
        norm_kernel,
        [((2, LOCAL), f32), ((LOCAL, 2), f32)],
        (w_dec,),
        [hbm],
        [pltpu.VMEM((LOCAL, WIDTH), bf16), pltpu.SemaphoreType.DMA((4,))],
        flops=4 * LOCAL * WIDTH,
        nbytes=8 * MIB,
    )
    x_own, norm_row, norm_col = lax.optimization_barrier((chips(block), norm_row, norm_col))
    x_own = x_own.reshape(ROWS, HALF + PAD)
    x_other = swap(x_own)
    acc, w_rest, mask, home_own, *xs = call(
        encode_own_kernel,
        [((ROWS, LOCAL), f32), ((HALF, LOCAL), bf16, pltpu.VMEM), ((ROWS, PAD), bf16)] + [((ROWS, SUB), bf16)] * 4,
        (x_own, w_enc),
        [VM, hbm],
        [pltpu.VMEM((HALF, LOCAL), bf16), pltpu.SemaphoreType.DMA((8,))],
        flops=half_flops,
        nbytes=10 * MIB,
    )
    act, feats, part_send, home_other = call(
        encode_kernel,
        [((ROWS, LOCAL), f32), ((ROWS + 16, LOCAL), bf16), ((ROWS, HALF), bf16), ((ROWS, SUB), bf16)],
        (x_other, mask, acc, b_enc.reshape(1, LOCAL), w_rest, w_dec),
        [VM] * 5 + [hbm],
        dec_scratch,
        flops=2 * half_flops,
        nbytes=8 * MIB,
    )
    part_recv = swap(part_send)
    (part_own,) = call(
        decode_own_kernel,
        [((ROWS, HALF), f32)],
        (feats, w_dec),
        [VM, hbm],
        dec_scratch,
        flops=half_flops,
        nbytes=6 * MIB,
    )
    (part,) = call(add_kernel, [((ROWS, HALF), bf16)], (part_own, part_recv), vmem=8 * MIB)
    parts = chips(part.reshape(CHIPS, 8, HALF))
    xs = [shift(xs[k - 1], k) for k in range(1, NZ)]
    (block,) = call(
        err_kernel,
        [((CHIPS, 8, HALF + PAD), bf16)],
        (parts, mine, b_dec, feats, norm_row),
    )
    block, *xs = lax.optimization_barrier((block, *xs))
    (xs,) = call(merge_kernel, [((3 * ROWS, SUB), bf16)], xs, nbytes=2 * MIB)
    fs = [feats] + [shift(feats, k) for k in range(1, NZ)]
    e_own, xs, xs_other, *fs = lax.optimization_barrier((chips(block), xs, swap(xs), *fs))
    e_own = e_own.reshape(ROWS, HALF + PAD)
    e_other = swap(e_own)
    slices = call(slice_kernel, [((ROWS, SUB), bf16)] * 3, (e_own,), nbytes=MIB)
    es = [shift(slices[k - 1], k) for k in range(1, NZ)]
    (dpre,) = call(
        dpre_kernel,
        [((ROWS + 16, LOCAL), bf16)],
        (e_own, e_other, mask, norm_row, at_hbm(act), w_dec),
        [VM] * 4 + [hbm] * 2,
        [
            pltpu.VMEM((ROWS, LOCAL), f32),
            pltpu.VMEM((2, NZ, LOCAL, SUB), bf16),
            pltpu.SemaphoreType.DMA,
            pltpu.SemaphoreType.DMA((8,)),
        ],
        flops=2 * half_flops,
        nbytes=10 * MIB,
    )
    ds = [dpre] + [shift(dpre, k) for k in range(1, NZ)]
    xt, ft, scale, count, w_slice = call(
        turn_kernel,
        [
            ((2, SUB, NZ * ROWS), bf16),
            ((LOCAL, NZ * ROWS), bf16),
            ((LOCAL, 1), f32),
            ((1, 1), f32),
            ((LOCAL, 2 * SUB), bf16),
        ],
        (home_own, home_other, xs, xs_other, *fs, norm_col, w_dec, dpre),
        [VM] * 9 + [hbm, anywhere],
        [pltpu.SemaphoreType.DMA],
        nbytes=6 * MIB,
    )
    es, ds, loss = call(
        part_kernel,
        [((3 * ROWS, SUB), bf16), ((NZ * ROWS, LOCAL), bf16), ((1, 1), f32)],
        (*ds, *es, count),
        nbytes=3 * MIB,
    )
    (grad_enc,) = call(
        grad_enc_kernel,
        [((2, SUB, LOCAL), bf16)],
        (xt, count, ds),
        scratch=[pltpu.VMEM((2, SUB, LOCAL), bf16), pltpu.SemaphoreType.DMA((4,))],
        out_specs=[hbm],
        flops=4 * half_flops,
        nbytes=5 * MIB,
    )
    (grad_dec,) = call(
        grad_dec_kernel,
        [((LOCAL, 2 * SUB), bf16)],
        (e_own, e_other, es, swap(es), ft, scale, count, w_slice),
        scratch=[
            pltpu.VMEM((NZ * ROWS, 2 * SUB), bf16),
            pltpu.VMEM((LOCAL, 2 * SUB), bf16),
            pltpu.SemaphoreType.DMA((4,)),
        ],
        out_specs=[hbm],
        flops=4 * half_flops,
        nbytes=7 * MIB,
    )
    return grad_enc, grad_dec, loss.reshape(())


def solution(mesh):
    fine = Mesh(mesh.devices.reshape(4, 4, 4, 2), ALL)
    lat = ("x", "y", "c")
    return jax.shard_map(
        shards,
        mesh=fine,
        in_specs=(P(ALL, None), P(ALL), P(ALL, None), P(None, None, lat), P(lat), P(lat, None), P()),
        out_specs=(P(None, "z", lat), P(lat, "z"), P()),
        check_vma=False,
    )
```

```python
import jax
import jax.numpy as jnp
from jax import lax
from jax.experimental import pallas as pl
from jax.experimental.pallas import tpu as pltpu
from jax.sharding import Mesh
from jax.sharding import PartitionSpec as P

sparsity_weight = 1.0
loss_scale = 8.0
norm_eps = 1e-06

ALL = ("z", "x", "y", "c")
NZ = 4
CHIPS = 16
WIDTH = 8192
HALF = 4096
SUB = 1024
LOCAL = 512
ROWS = 128
PAD = 128
MIB = 1 << 20
f32 = jnp.float32
bf16 = jnp.bfloat16

VM = pl.BlockSpec(memory_space=pltpu.VMEM)


def at_hbm(v):
    return pltpu.with_memory_space_constraint(v, pltpu.HBM)


def call(body, outs, args, specs=None, scratch=(), vmem=None, flops=0, nbytes=0, out_specs=None, aliases=None):
    return pl.pallas_call(
        body,
        out_shape=[o[2](o[0], o[1]) if len(o) == 3 else jax.ShapeDtypeStruct(*o) for o in outs],
        in_specs=specs or [VM] * len(args),
        out_specs=out_specs or [VM] * len(outs),
        scratch_shapes=list(scratch),
        input_output_aliases=aliases or {},
        compiler_params=pltpu.CompilerParams(vmem_limit_bytes=vmem or 16 * MIB),
        cost_estimate=pl.CostEstimate(flops=flops, bytes_accessed=nbytes, transcendentals=0),
    )(*args)


def lanes(start, size):
    return pl.ds(pl.multiple_of(start, 128), size)


def split3(v):
    hi = v.astype(bf16)
    rest = v - hi.astype(f32)
    mid = rest.astype(bf16)
    low = (rest - mid.astype(f32)).astype(bf16)
    return hi, mid, low


def prep_kernel(length, acts_hbm, group_hbm, keep, send, acts, group, sems):
    copies = [
        pltpu.make_async_copy(src, dst, sems.at[i])
        for i, (src, dst) in enumerate(((acts_hbm, acts), (group_hbm, group)))
    ]
    for copy in copies:
        copy.start()
    for copy in copies:
        copy.wait()
    c = lax.axis_index("c")
    slot = lax.broadcasted_iota(jnp.int32, (1, 5), 1)
    held = jnp.sum(jnp.where(group[...] == NZ, slot, 0), axis=1, keepdims=True)
    k = lax.broadcasted_iota(jnp.int32, (4, 1), 0)
    later = k >= held
    src = k + later.astype(jnp.int32)
    live = (src < length[0]).astype(f32)
    live = jnp.broadcast_to(live, (4, PAD)).astype(bf16)

    def pick(cols):
        rows = acts[:, cols].astype(f32)
        return jnp.where(later, rows[1:5], rows[0:4]).astype(bf16)

    for out, core in ((keep, c), (send, 1 - c)):
        out[:, :HALF] = pick(lanes(core * HALF, HALF))
        for q in range(NZ):
            out[:, HALF + q * SUB : HALF + (q + 1) * SUB] = pick(lanes(q * 2 * SUB + core * SUB, SUB))
        out[:, 2 * HALF :] = live


def join_kernel(own, other, out, mine):
    first = lax.axis_index("c") == 0
    a, b = own[...].astype(f32), other[...].astype(f32)
    rows = jnp.concatenate([jnp.where(first, a, b), jnp.where(first, b, a)], axis=0)
    mine[...] = rows[:, HALF:].astype(bf16)
    for i in range(CHIPS):
        out[i, :, :HALF] = rows[:, :HALF].astype(bf16)
        out[i, :, HALF:] = rows[:, 2 * HALF :].astype(bf16)


def norm_kernel(w_dec_hbm, norm_row, norm_col, w_dec, sems):
    rows = LOCAL // 4
    copies = [
        pltpu.make_async_copy(w_dec_hbm.at[pl.ds(i * rows, rows)], w_dec.at[pl.ds(i * rows, rows)], sems.at[i])
        for i in range(4)
    ]
    for copy in copies:
        copy.start()
    for i in range(4):
        copies[i].wait()
        n = i * rows
        for s in range(2):

            def add(j, total):
                for m in range(4):
                    v = w_dec[n : n + rows, lanes(s * HALF + j * 512 + m * 128, 128)].astype(f32)
                    total = total + v * v
                return total

            total = lax.fori_loop(0, HALF // 512, add, jnp.zeros((rows, 128), f32))
            norm_row[s : s + 1, n : n + rows] = jnp.sqrt(jnp.sum(total.T, axis=0, keepdims=True) + norm_eps)
            norm_col[n : n + rows, s : s + 1] = jnp.sqrt(jnp.sum(total, axis=1, keepdims=True) + norm_eps)


def fetch_enc(w_hbm, core, buf, sems, at=0):
    copies = [
        pltpu.make_async_copy(w_hbm.at[core, pl.ds(i * SUB, SUB)], buf.at[pl.ds(i * SUB, SUB)], sems.at[at + i])
        for i in range(4)
    ]
    for copy in copies:
        copy.start()
    return copies


def fetch_dec(w_hbm, core, buf, sems, at=0):
    copies = [
        pltpu.make_async_copy(w_hbm.at[:, lanes(q * 2 * SUB + core * SUB, SUB)], buf.at[q], sems.at[at + q])
        for q in range(NZ)
    ]
    for copy in copies:
        copy.start()
    return copies


def encode_own_kernel(x, w_enc, acc, rest, mask, home, p1, p2, p3, buf, sems, out_sems):
    z, c = lax.axis_index("z"), lax.axis_index("c")
    copies = fetch_enc(w_enc, c, buf, sems)
    later = fetch_enc(w_enc, 1 - c, rest, sems, 4)
    for k, out in enumerate((home, p1, p2, p3)):
        piece = x.at[:, lanes(lax.rem(z + k, NZ) * SUB, SUB)]
        later.append(pltpu.make_async_copy(piece, out, out_sems.at[k]))
        later[-1].start()
    mask[...] = x[:, HALF:]
    for i in range(0, 4, 2):
        copies[i].wait()
        copies[i + 1].wait()
        rows = slice(i * SUB, (i + 2) * SUB)
        for n in range(0, LOCAL, 256):
            part = jnp.dot(x[:, rows], buf[rows, n : n + 256], preferred_element_type=f32)
            acc[:, n : n + 256] = part if i == 0 else acc[:, n : n + 256] + part
    for copy in later:
        copy.wait()


def encode_kernel(x, mask, part, bias, w_enc, w_dec, act_hbm, feats_out, send, home, act_out, dec, dec_sems, out_sems):
    z, c = lax.axis_index("z"), lax.axis_index("c")
    dec_copies = fetch_dec(w_dec, 1 - c, dec, dec_sems)
    later = [pltpu.make_async_copy(x.at[:, lanes(z * SUB, SUB)], home, out_sems.at[0])]
    later[0].start()
    live = mask[:, 0:1].astype(f32)
    count = jnp.sum(live, axis=0, keepdims=True)
    for n in range(0, LOCAL, 256):
        pre = part[:, n : n + 256] + jnp.dot(x[:, :HALF], w_enc[:, n : n + 256], preferred_element_type=f32)
        act = jnp.maximum(pre + bias[:, n : n + 256], 0.0)
        feats = act * act
        act_out[:, n : n + 256] = act
        feats_out[:ROWS, n : n + 256] = feats.astype(bf16)
        fsum = jnp.sum(feats * live, axis=0, keepdims=True)
        tail = jnp.zeros((8, 256), f32)
        row = lax.broadcasted_iota(jnp.int32, (8, 256), 0)
        for i, piece in enumerate((*split3(fsum), jnp.broadcast_to(count, (1, 256)))):
            tail = jnp.where(row == i, piece.astype(f32), tail)
        feats_out[ROWS:, n : n + 256] = tail.astype(bf16)
    later.append(pltpu.make_async_copy(act_out, act_hbm, out_sems.at[1]))
    later[1].start()
    feats16 = feats_out[:ROWS, :]
    for q in range(NZ):
        dec_copies[q].wait()
        send[:, q * SUB : (q + 1) * SUB] = jnp.dot(feats16, dec[q], preferred_element_type=f32).astype(bf16)
    for copy in later:
        copy.wait()


def decode_own_kernel(feats, w_dec, part, buf, sems):
    copies = fetch_dec(w_dec, lax.axis_index("c"), buf, sems)
    feats16 = feats[:ROWS, :]
    for q in range(NZ):
        copies[q].wait()
        part[:, q * SUB : (q + 1) * SUB] = jnp.dot(feats16, buf[q], preferred_element_type=f32)


def turn_kernel(home_own, home_other, own, other, *refs):
    z, c = lax.axis_index("z"), lax.axis_index("c")
    feats, norm_col, w_dec = refs[0:4], refs[4], refs[5]
    xt, ft, scale, count, w, sem = refs[7:]
    fetch = pltpu.make_async_copy(w_dec.at[:, lanes(z * 2 * SUB, 2 * SUB)], w, sem)
    fetch.start()
    fsum = jnp.zeros((1, LOCAL), f32)
    total = jnp.zeros((1, 1), f32)
    for side, mine, rest in ((c, home_own, own), (1 - c, home_other, other)):
        xt[side, :, :ROWS] = mine[...].T
        for k in range(1, NZ):
            xt[side, :, k * ROWS : (k + 1) * ROWS] = rest[(k - 1) * ROWS : k * ROWS, :].T
    for k in range(NZ):
        ft[:, k * ROWS : (k + 1) * ROWS] = feats[k][:ROWS, :].T
        fsum = fsum + jnp.sum(feats[k][ROWS : ROWS + 3, :].astype(f32), axis=0, keepdims=True)
        total = total + feats[k][ROWS + 3 : ROWS + 4, 0:1].astype(f32)
    count[...] = total
    fsum = jnp.broadcast_to(fsum, (128, LOCAL)).T[:, 0:1]
    norm = jnp.where(z < 2, norm_col[:, 0:1], norm_col[:, 1:2])
    scale[...] = sparsity_weight * fsum / norm
    fetch.wait()


def add_kernel(own, other, out, total, sems):
    copies = []
    for i in range(4):
        rows = slice(i * 32, (i + 1) * 32)
        total[rows, :] = (own[rows, :] + other[rows, :].astype(f32)).astype(bf16)
        copies.append(pltpu.make_async_copy(total.at[pl.ds(i * 32, 32)], out.at[pl.ds(i * 32, 32)], sems.at[i]))
        copies[-1].start()
    for copy in copies:
        copy.wait()


def err_kernel(parts, mine, bias, feats, norm_row, out_hbm, out, sems):
    c = lax.axis_index("c")
    live = mine[:, HALF : HALF + 1].astype(f32)
    square = jnp.zeros((8, SUB), f32)
    copies = []
    for q in range(NZ):
        cols = slice(q * SUB, (q + 1) * SUB)
        total = parts[0, :, cols].astype(f32)
        for i in range(1, CHIPS):
            total = total + parts[i, :, cols].astype(f32)
        add = bias[q // 2 : q // 2 + 1, lanes((q % 2) * 2 * SUB + c * SUB, SUB)]
        err = (total + add - mine[:, cols].astype(f32)) * live
        square = square + err * err
        err16 = err.astype(bf16)
        for i in range(CHIPS):
            out[i, :, cols] = err16
        piece = pl.ds(q * SUB, SUB)
        copies.append(pltpu.make_async_copy(out.at[:, :, piece], out_hbm.at[:, :, piece], sems.at[q]))
        copies[-1].start()
    squares = jnp.sum(jnp.sum(square, axis=0, keepdims=True), axis=1, keepdims=True)
    fsum = jnp.sum(feats[ROWS : ROWS + 3, :].astype(f32), axis=0, keepdims=True)
    nsum = norm_row[0:1, :] + norm_row[1:2, :]
    sparse = sparsity_weight * jnp.sum(fsum * nsum, axis=1, keepdims=True)
    lane = lax.broadcasted_iota(jnp.int32, (8, PAD), 1)
    row = lax.broadcasted_iota(jnp.int32, (8, PAD), 0)
    tail = jnp.zeros((8, PAD), f32)
    for i, piece in enumerate(split3(squares + sparse)):
        tail = jnp.where((lane == i) & (row == 0), piece.astype(f32), tail)
    for i in range(CHIPS):
        out[i, :, HALF:] = tail.astype(bf16)
    piece = pl.ds(HALF, PAD)
    copies.append(pltpu.make_async_copy(out.at[:, :, piece], out_hbm.at[:, :, piece], sems.at[NZ]))
    copies[-1].start()
    for copy in copies:
        copy.wait()


def slice_kernel(e, s1, s2, s3):
    z = lax.axis_index("z")
    for k, out in enumerate((s1, s2, s3)):
        out[...] = e[:, lanes(lax.rem(z + k + 1, NZ) * SUB, SUB)]


def dpre_kernel(own, e, mask, norm_row, act_hbm, w_dec, out, act, buf, act_sem, sems):
    c = lax.axis_index("c")
    copies = fetch_dec(w_dec, c, buf.at[0], sems) + fetch_dec(w_dec, 1 - c, buf.at[1], sems, 4)
    fetch = pltpu.make_async_copy(act_hbm, act, act_sem)
    fetch.start()
    both = e[:, HALF:].astype(f32) + own[:, HALF:].astype(f32)
    both = jnp.sum(jnp.sum(both, axis=0, keepdims=True), axis=1, keepdims=True)
    lane = lax.broadcasted_iota(jnp.int32, (8, LOCAL), 1)
    tail = jnp.zeros((8, LOCAL), f32)
    for i, piece in enumerate(split3(both)):
        tail = jnp.where(lane == i, piece.astype(f32), tail)
    out[ROWS:, :] = tail.astype(bf16)
    live = mask[:, 0:1].astype(f32)
    totals = [jnp.zeros((ROWS, 256), f32), jnp.zeros((ROWS, 256), f32)]
    for q in range(2 * NZ):
        copies[q].wait()
        rows = (own, e)[q // NZ]
        for i in range(2):
            totals[i] = totals[i] + lax.dot_general(
                rows[:, (q % NZ) * SUB : (q % NZ + 1) * SUB],
                buf[q // NZ, q % NZ, i * 256 : (i + 1) * 256, :],
                (((1,), (1,)), ((), ())),
                preferred_element_type=f32,
            )
    fetch.wait()
    for i in range(2):
        n = slice(i * 256, (i + 1) * 256)
        nsum = norm_row[0:1, n] + norm_row[1:2, n]
        grad = 2.0 * totals[i] + sparsity_weight * live * nsum
        out[:ROWS, n] = (grad * 2.0 * act[:, n]).astype(bf16)


def merge_kernel(a, b, d, out):
    for k, v in enumerate((a, b, d)):
        out[k * ROWS : (k + 1) * ROWS, :] = v[...]


def part_kernel(*refs):
    pres, slices, count = refs[0:4], refs[4:7], refs[7]
    es, ds, loss = refs[8:]
    total = jnp.zeros((1, 1), f32)
    for k, p in enumerate(pres):
        total = total + jnp.sum(p[ROWS : ROWS + 1, 0:3].astype(f32), axis=1, keepdims=True)
        ds[k * ROWS : (k + 1) * ROWS, :] = p[:ROWS, :]
    for k, p in enumerate(slices):
        es[k * ROWS : (k + 1) * ROWS, :] = p[...]
    loss[...] = total / (count[...] * WIDTH)


def dec_half(side, plane, rest, ft, scale, w, factor, done, rows):
    z = lax.axis_index("z")
    for m in range(0, SUB, 512):
        part = jnp.dot(ft[rows, :ROWS], plane[:, lanes(z * SUB + m, 512)], preferred_element_type=f32)
        part = part + jnp.dot(ft[rows, ROWS:], rest[:, m : m + 512], preferred_element_type=f32)
        part = part * (2.0 * factor) + (scale[rows, :] * factor) * w[rows, lanes(side * SUB + m, 512)].astype(f32)
        done[rows, m : m + 512] = part.astype(bf16)


def copy_dec(side, done, out, sem, rows):
    copy = pltpu.make_async_copy(done.at[rows], out.at[rows, lanes(side * SUB, SUB)], sem)
    copy.start()
    return copy


def grads_kernel(xt, count, ds, e_own, own, ft, scale, w, out_enc, out_dec, done, done_dec, sems):
    c = lax.axis_index("c")
    factor = loss_scale / count[...]
    copies = []
    for i in range(4):
        rows = pl.ds(i % 2 * 512, 512)
        for n in range(0, 512, 256):
            at = i % 2 * 512 + n
            part = jnp.dot(xt[i // 2, at : at + 256, :], ds[...], preferred_element_type=f32)
            done[i // 2, at : at + 256, :] = (part * factor).astype(bf16)
        copies.append(pltpu.make_async_copy(done.at[i // 2, rows], out_enc.at[i // 2, rows], sems.at[i]))
        copies[-1].start()
    for i in range(2):
        for n in range(i * 256, i * 256 + 256, 128):
            dec_half(c, e_own, own, ft, scale, w, factor, done_dec, pl.ds(n, 128))
        copies.append(copy_dec(c, done_dec, out_dec, sems.at[4 + i], pl.ds(i * 256, 256)))
    for copy in copies:
        copy.wait()


def rest_kernel(e_other, other, ft, scale, count, w, half, out, done, sems):
    del half
    side = 1 - lax.axis_index("c")
    factor = loss_scale / count[...]
    copies = []
    for i in range(2):
        for n in range(i * 256, i * 256 + 256, 128):
            dec_half(side, e_other, other, ft, scale, w, factor, done, pl.ds(n, 128))
        copies.append(copy_dec(side, done, out, sems.at[i], pl.ds(i * 256, 256)))
    for copy in copies:
        copy.wait()


def swap(v):
    return lax.ppermute(v, "c", [(0, 1), (1, 0)])


def chips(v):
    return lax.all_to_all(v, ("x", "y"), split_axis=0, concat_axis=0, tiled=True)


def planes(v):
    return lax.all_to_all(v, "z", split_axis=0, concat_axis=0, tiled=True)


def shift(v, k):
    return lax.ppermute(v, "z", [(i, (i + k) % NZ) for i in range(NZ)])


def shards(acts, chat_len, group_of, w_enc, b_enc, w_dec, b_dec):
    half_flops = 2 * ROWS * HALF * LOCAL
    w_enc, w_dec = at_hbm(w_enc), at_hbm(w_dec)
    dec_scratch = [pltpu.VMEM((4, LOCAL, SUB), bf16), pltpu.SemaphoreType.DMA((4,))]
    hbm = pl.BlockSpec(memory_space=pltpu.HBM)
    anywhere = pl.BlockSpec(memory_space=pl.ANY)
    keep, send = call(
        prep_kernel,
        [((4, 2 * HALF + PAD), bf16)] * 2,
        (chat_len, at_hbm(acts), at_hbm(group_of.reshape(1, 5))),
        [pl.BlockSpec(memory_space=pltpu.SMEM), hbm, hbm],
        [
            pltpu.VMEM((5, WIDTH), bf16),
            pltpu.VMEM((1, 5), jnp.int32),
            pltpu.SemaphoreType.DMA((2,)),
        ],
        vmem=4 * MIB,
    )
    block, mine = call(
        join_kernel,
        [((CHIPS, 8, HALF + PAD), bf16), ((8, HALF + PAD), bf16)],
        (keep, swap(send)),
        vmem=4 * MIB,
    )
    x_own = chips(block).reshape(ROWS, HALF + PAD)
    x_other = swap(x_own)
    acc, w_rest, mask, home_own, *xs = call(
        encode_own_kernel,
        [((ROWS, LOCAL), f32), ((HALF, LOCAL), bf16, pltpu.VMEM), ((ROWS, PAD), bf16)]
        + [((ROWS, SUB), bf16, pltpu.HBM)] * 4,
        (x_own, w_enc),
        [VM, hbm],
        [pltpu.VMEM((HALF, LOCAL), bf16), pltpu.SemaphoreType.DMA((8,)), pltpu.SemaphoreType.DMA((4,))],
        out_specs=[VM] * 3 + [hbm] * 4,
        flops=half_flops,
        nbytes=10 * MIB,
    )
    act, feats, part_send, home_other = call(
        encode_kernel,
        [
            ((ROWS, LOCAL), f32, pltpu.HBM),
            ((ROWS + 8, LOCAL), bf16),
            ((ROWS, HALF), bf16),
            ((ROWS, SUB), bf16, pltpu.HBM),
        ],
        (x_other, mask, acc, b_enc.reshape(1, LOCAL), w_rest, w_dec),
        [VM] * 5 + [hbm],
        [pltpu.VMEM((ROWS, LOCAL), f32), *dec_scratch, pltpu.SemaphoreType.DMA((2,))],
        out_specs=[hbm, VM, VM, hbm],
        flops=2 * half_flops,
        nbytes=8 * MIB,
    )
    part_recv = swap(part_send)
    (part_own,) = call(
        decode_own_kernel,
        [((ROWS, HALF), f32)],
        (feats, w_dec),
        [VM, hbm],
        dec_scratch,
        flops=half_flops,
        nbytes=6 * MIB,
    )
    (part,) = call(
        add_kernel,
        [((ROWS, HALF), bf16, pltpu.HBM)],
        (part_own, part_recv),
        scratch=[pltpu.VMEM((ROWS, HALF), bf16), pltpu.SemaphoreType.DMA((4,))],
        out_specs=[hbm],
        vmem=8 * MIB,
    )
    norm_row, norm_col = call(
        norm_kernel,
        [((2, LOCAL), f32), ((LOCAL, 2), f32)],
        (w_dec,),
        [hbm],
        [pltpu.VMEM((LOCAL, WIDTH), bf16), pltpu.SemaphoreType.DMA((4,))],
        flops=4 * LOCAL * WIDTH,
        nbytes=8 * MIB,
    )
    parts, norm_row, norm_col = lax.optimization_barrier((chips(part.reshape(CHIPS, 8, HALF)), norm_row, norm_col))
    xs = [shift(xs[k - 1], k) for k in range(1, NZ)]
    (block,) = call(
        err_kernel,
        [((CHIPS, 8, HALF + PAD), bf16, pltpu.HBM)],
        (parts, mine, b_dec, feats, norm_row),
        scratch=[pltpu.VMEM((CHIPS, 8, HALF + PAD), bf16), pltpu.SemaphoreType.DMA((NZ + 1,))],
        out_specs=[hbm],
    )
    block, *xs = lax.optimization_barrier((block, *xs))
    (xs,) = call(merge_kernel, [((3 * ROWS, SUB), bf16)], xs, nbytes=2 * MIB)
    fs = [feats] + [shift(feats, k) for k in range(1, NZ)]
    e_own, xs, xs_other, *fs = lax.optimization_barrier((chips(block), xs, swap(xs), *fs))
    e_own = e_own.reshape(ROWS, HALF + PAD)
    e_other = swap(e_own)
    slices = call(slice_kernel, [((ROWS, SUB), bf16)] * 3, (e_own,), nbytes=MIB)
    es = [shift(slices[k - 1], k) for k in range(1, NZ)]
    (dpre,) = call(
        dpre_kernel,
        [((ROWS + 8, LOCAL), bf16)],
        (e_own, e_other, mask, norm_row, at_hbm(act), w_dec),
        [VM] * 4 + [hbm] * 2,
        [
            pltpu.VMEM((ROWS, LOCAL), f32),
            pltpu.VMEM((2, NZ, LOCAL, SUB), bf16),
            pltpu.SemaphoreType.DMA,
            pltpu.SemaphoreType.DMA((8,)),
        ],
        flops=2 * half_flops,
        nbytes=10 * MIB,
    )
    ds = [dpre] + [shift(dpre, k) for k in range(1, NZ)]
    xt, ft, scale, count, w_slice = call(
        turn_kernel,
        [
            ((2, SUB, NZ * ROWS), bf16),
            ((LOCAL, NZ * ROWS), bf16),
            ((LOCAL, 1), f32),
            ((1, 1), f32),
            ((LOCAL, 2 * SUB), bf16),
        ],
        (home_own, home_other, xs, xs_other, *fs, norm_col, w_dec, dpre),
        [VM] * 9 + [hbm, anywhere],
        [pltpu.SemaphoreType.DMA],
        nbytes=6 * MIB,
    )
    es, ds, loss = call(
        part_kernel,
        [((3 * ROWS, SUB), bf16), ((NZ * ROWS, LOCAL), bf16), ((1, 1), f32)],
        (*ds, *es, count),
        nbytes=3 * MIB,
    )
    grad_enc, half = call(
        grads_kernel,
        [((2, SUB, LOCAL), bf16), ((LOCAL, 2 * SUB), bf16)],
        (xt, count, ds, e_own, es, ft, scale, w_slice),
        scratch=[
            pltpu.VMEM((2, SUB, LOCAL), bf16),
            pltpu.VMEM((LOCAL, SUB), bf16),
            pltpu.SemaphoreType.DMA((6,)),
        ],
        out_specs=[hbm, hbm],
        flops=6 * half_flops,
        nbytes=8 * MIB,
    )
    (grad_dec,) = call(
        rest_kernel,
        [((LOCAL, 2 * SUB), bf16)],
        (e_other, swap(es), ft, scale, count, w_slice, half),
        [VM] * 6 + [hbm],
        [pltpu.VMEM((LOCAL, SUB), bf16), pltpu.SemaphoreType.DMA((2,))],
        out_specs=[hbm],
        aliases={6: 0},
        flops=2 * half_flops,
        nbytes=3 * MIB,
    )
    return grad_enc, grad_dec, loss.reshape(())


def solution(mesh):
    fine = Mesh(mesh.devices.reshape(4, 4, 4, 2), ALL)
    lat = ("x", "y", "c")
    return jax.shard_map(
        shards,
        mesh=fine,
        in_specs=(P(ALL, None), P(ALL), P(ALL, None), P(None, None, lat), P(lat), P(lat, None), P()),
        out_specs=(P(None, "z", lat), P(lat, "z"), P()),
        check_vma=False,
    )
```

```python
import jax
import jax.numpy as jnp
from jax import lax
from jax.experimental import pallas as pl
from jax.experimental.pallas import tpu as pltpu
from jax.sharding import Mesh
from jax.sharding import PartitionSpec as P

sparsity_weight = 1.0
loss_scale = 8.0
norm_eps = 1e-06

ALL = ("z", "x", "y", "c")
NZ = 4
CHIPS = 16
WIDTH = 8192
HALF = 4096
SUB = 1024
LOCAL = 512
ROWS = 128
PAD = 128
MIB = 1 << 20
f32 = jnp.float32
bf16 = jnp.bfloat16

VM = pl.BlockSpec(memory_space=pltpu.VMEM)


def at_hbm(v):
    return pltpu.with_memory_space_constraint(v, pltpu.HBM)


def call(body, outs, args, specs=None, scratch=(), vmem=None, flops=0, nbytes=0, out_specs=None, aliases=None):
    return pl.pallas_call(
        body,
        out_shape=[o[2](o[0], o[1]) if len(o) == 3 else jax.ShapeDtypeStruct(*o) for o in outs],
        in_specs=specs or [VM] * len(args),
        out_specs=out_specs or [VM] * len(outs),
        scratch_shapes=list(scratch),
        input_output_aliases=aliases or {},
        compiler_params=pltpu.CompilerParams(vmem_limit_bytes=vmem or 16 * MIB),
        cost_estimate=pl.CostEstimate(flops=flops, bytes_accessed=nbytes, transcendentals=0),
    )(*args)


def lanes(start, size):
    return pl.ds(pl.multiple_of(start, 128), size)


def split3(v):
    hi = v.astype(bf16)
    rest = v - hi.astype(f32)
    mid = rest.astype(bf16)
    low = (rest - mid.astype(f32)).astype(bf16)
    return hi, mid, low


def prep_kernel(length, acts_hbm, group_hbm, keep, send, acts, group, sems):
    copies = [
        pltpu.make_async_copy(src, dst, sems.at[i])
        for i, (src, dst) in enumerate(((acts_hbm, acts), (group_hbm, group)))
    ]
    for copy in copies:
        copy.start()
    for copy in copies:
        copy.wait()
    c = lax.axis_index("c")
    slot = lax.broadcasted_iota(jnp.int32, (1, 5), 1)
    held = jnp.sum(jnp.where(group[...] == NZ, slot, 0), axis=1, keepdims=True)
    k = lax.broadcasted_iota(jnp.int32, (4, 1), 0)
    later = k >= held
    src = k + later.astype(jnp.int32)
    live = (src < length[0]).astype(f32)
    live = jnp.broadcast_to(live, (4, PAD)).astype(bf16)

    def pick(cols):
        rows = acts[:, cols].astype(f32)
        return jnp.where(later, rows[1:5], rows[0:4]).astype(bf16)

    for out, core in ((keep, c), (send, 1 - c)):
        out[:, :HALF] = pick(lanes(core * HALF, HALF))
        for q in range(NZ):
            out[:, HALF + q * SUB : HALF + (q + 1) * SUB] = pick(lanes(q * 2 * SUB + core * SUB, SUB))
        out[:, 2 * HALF :] = live


def join_kernel(own, other, out, mine):
    first = lax.axis_index("c") == 0
    a, b = own[...].astype(f32), other[...].astype(f32)
    rows = jnp.concatenate([jnp.where(first, a, b), jnp.where(first, b, a)], axis=0)
    mine[...] = rows[:, HALF:].astype(bf16)
    for i in range(CHIPS):
        out[i, :, :HALF] = rows[:, :HALF].astype(bf16)
        out[i, :, HALF:] = rows[:, 2 * HALF :].astype(bf16)


def norm_kernel(w_dec_hbm, norm_row, norm_col, w_dec, sems):
    rows = LOCAL // 4
    copies = [
        pltpu.make_async_copy(w_dec_hbm.at[pl.ds(i * rows, rows)], w_dec.at[pl.ds(i * rows, rows)], sems.at[i])
        for i in range(4)
    ]
    for copy in copies:
        copy.start()
    for i in range(4):
        copies[i].wait()
        n = i * rows
        for s in range(2):

            def add(j, total):
                for m in range(4):
                    v = w_dec[n : n + rows, lanes(s * HALF + j * 512 + m * 128, 128)].astype(f32)
                    total = total + v * v
                return total

            total = lax.fori_loop(0, HALF // 512, add, jnp.zeros((rows, 128), f32))
            norm_row[s : s + 1, n : n + rows] = jnp.sqrt(jnp.sum(total.T, axis=0, keepdims=True) + norm_eps)
            norm_col[n : n + rows, s : s + 1] = jnp.sqrt(jnp.sum(total, axis=1, keepdims=True) + norm_eps)


def fetch_enc(w_hbm, core, buf, sems, at=0):
    copies = [
        pltpu.make_async_copy(w_hbm.at[core, pl.ds(i * SUB, SUB)], buf.at[pl.ds(i * SUB, SUB)], sems.at[at + i])
        for i in range(4)
    ]
    for copy in copies:
        copy.start()
    return copies


def fetch_dec(w_hbm, core, buf, sems, at=0):
    copies = [
        pltpu.make_async_copy(w_hbm.at[:, lanes(q * 2 * SUB + core * SUB, SUB)], buf.at[q], sems.at[at + q])
        for q in range(NZ)
    ]
    for copy in copies:
        copy.start()
    return copies


def encode_own_kernel(x, w_enc, acc, rest, mask, home, p1, p2, p3, buf, sems, out_sems):
    z, c = lax.axis_index("z"), lax.axis_index("c")
    copies = fetch_enc(w_enc, c, buf, sems)
    later = fetch_enc(w_enc, 1 - c, rest, sems, 4)
    for k, out in enumerate((home, p1, p2, p3)):
        piece = x.at[:, lanes(lax.rem(z + k, NZ) * SUB, SUB)]
        later.append(pltpu.make_async_copy(piece, out, out_sems.at[k]))
        later[-1].start()
    mask[...] = x[:, HALF:]
    for i in range(0, 4, 2):
        copies[i].wait()
        copies[i + 1].wait()
        rows = slice(i * SUB, (i + 2) * SUB)
        for n in range(0, LOCAL, 256):
            part = jnp.dot(x[:, rows], buf[rows, n : n + 256], preferred_element_type=f32)
            acc[:, n : n + 256] = part if i == 0 else acc[:, n : n + 256] + part
    for copy in later:
        copy.wait()


def encode_kernel(x, mask, part, bias, w_enc, w_dec, act_hbm, feats_out, send, home, act_out, dec, dec_sems, out_sems):
    z, c = lax.axis_index("z"), lax.axis_index("c")
    dec_copies = fetch_dec(w_dec, 1 - c, dec, dec_sems)
    later = [pltpu.make_async_copy(x.at[:, lanes(z * SUB, SUB)], home, out_sems.at[0])]
    later[0].start()
    live = mask[:, 0:1].astype(f32)
    count = jnp.sum(live, axis=0, keepdims=True)
    for n in range(0, LOCAL, 256):
        pre = part[:, n : n + 256] + jnp.dot(x[:, :HALF], w_enc[:, n : n + 256], preferred_element_type=f32)
        act = jnp.maximum(pre + bias[:, n : n + 256], 0.0)
        feats = act * act
        act_out[:, n : n + 256] = act
        feats_out[:ROWS, n : n + 256] = feats.astype(bf16)
        fsum = jnp.sum(feats * live, axis=0, keepdims=True)
        tail = jnp.zeros((8, 256), f32)
        row = lax.broadcasted_iota(jnp.int32, (8, 256), 0)
        for i, piece in enumerate((*split3(fsum), jnp.broadcast_to(count, (1, 256)))):
            tail = jnp.where(row == i, piece.astype(f32), tail)
        feats_out[ROWS:, n : n + 256] = tail.astype(bf16)
    later.append(pltpu.make_async_copy(act_out, act_hbm, out_sems.at[1]))
    later[1].start()
    feats16 = feats_out[:ROWS, :]
    for q in range(NZ):
        dec_copies[q].wait()
        send[:, q * SUB : (q + 1) * SUB] = jnp.dot(feats16, dec[q], preferred_element_type=f32).astype(bf16)
    for copy in later:
        copy.wait()


def decode_own_kernel(feats, w_dec, part, buf, sems):
    copies = fetch_dec(w_dec, lax.axis_index("c"), buf, sems)
    feats16 = feats[:ROWS, :]
    for q in range(NZ):
        copies[q].wait()
        part[:, q * SUB : (q + 1) * SUB] = jnp.dot(feats16, buf[q], preferred_element_type=f32)


def turn_kernel(home_own, home_other, own, other, *refs):
    z, c = lax.axis_index("z"), lax.axis_index("c")
    feats, norm_col, w_dec = refs[0:4], refs[4], refs[5]
    xt, ft, scale, count, w, sem = refs[7:]
    fetch = pltpu.make_async_copy(w_dec.at[:, lanes(z * 2 * SUB, 2 * SUB)], w, sem)
    fetch.start()
    fsum = jnp.zeros((1, LOCAL), f32)
    total = jnp.zeros((1, 1), f32)
    for side, mine, rest in ((c, home_own, own), (1 - c, home_other, other)):
        xt[side, :, :ROWS] = mine[...].T
        for k in range(1, NZ):
            xt[side, :, k * ROWS : (k + 1) * ROWS] = rest[(k - 1) * ROWS : k * ROWS, :].T
    for k in range(NZ):
        ft[:, k * ROWS : (k + 1) * ROWS] = feats[k][:ROWS, :].T
        fsum = fsum + jnp.sum(feats[k][ROWS : ROWS + 3, :].astype(f32), axis=0, keepdims=True)
        total = total + feats[k][ROWS + 3 : ROWS + 4, 0:1].astype(f32)
    count[...] = jnp.broadcast_to(total, (8, PAD))
    fsum = jnp.broadcast_to(fsum, (128, LOCAL)).T[:, 0:1]
    norm = jnp.where(z < 2, norm_col[:, 0:1], norm_col[:, 1:2])
    scale[...] = sparsity_weight * fsum / norm
    fetch.wait()


def add_kernel(own, other, out, total, sems):
    copies = []
    for i in range(4):
        rows = slice(i * 32, (i + 1) * 32)
        total[rows, :] = (own[rows, :] + other[rows, :].astype(f32)).astype(bf16)
        copies.append(pltpu.make_async_copy(total.at[pl.ds(i * 32, 32)], out.at[pl.ds(i * 32, 32)], sems.at[i]))
        copies[-1].start()
    for copy in copies:
        copy.wait()


def err_kernel(parts, mine, bias, feats, norm_row, out_hbm, out, sems):
    c = lax.axis_index("c")
    live = mine[:, HALF : HALF + 1].astype(f32)
    square = jnp.zeros((8, SUB), f32)
    copies = []
    for q in range(NZ):
        cols = slice(q * SUB, (q + 1) * SUB)
        total = parts[0, :, cols].astype(f32)
        for i in range(1, CHIPS):
            total = total + parts[i, :, cols].astype(f32)
        add = bias[q // 2 : q // 2 + 1, lanes((q % 2) * 2 * SUB + c * SUB, SUB)]
        err = (total + add - mine[:, cols].astype(f32)) * live
        square = square + err * err
        err16 = err.astype(bf16)
        for i in range(CHIPS):
            out[i, :, cols] = err16
        piece = pl.ds(q * SUB, SUB)
        copies.append(pltpu.make_async_copy(out.at[:, :, piece], out_hbm.at[:, :, piece], sems.at[q]))
        copies[-1].start()
    squares = jnp.sum(jnp.sum(square, axis=0, keepdims=True), axis=1, keepdims=True)
    fsum = jnp.sum(feats[ROWS : ROWS + 3, :].astype(f32), axis=0, keepdims=True)
    nsum = norm_row[0:1, :] + norm_row[1:2, :]
    sparse = sparsity_weight * jnp.sum(fsum * nsum, axis=1, keepdims=True)
    lane = lax.broadcasted_iota(jnp.int32, (8, PAD), 1)
    row = lax.broadcasted_iota(jnp.int32, (8, PAD), 0)
    tail = jnp.zeros((8, PAD), f32)
    for i, piece in enumerate(split3(squares + sparse)):
        tail = jnp.where((lane == i) & (row == 0), piece.astype(f32), tail)
    for i in range(CHIPS):
        out[i, :, HALF:] = tail.astype(bf16)
    piece = pl.ds(HALF, PAD)
    copies.append(pltpu.make_async_copy(out.at[:, :, piece], out_hbm.at[:, :, piece], sems.at[NZ]))
    copies[-1].start()
    for copy in copies:
        copy.wait()


def slice_kernel(e, s1, s2, s3):
    z = lax.axis_index("z")
    for k, out in enumerate((s1, s2, s3)):
        out[...] = e[:, lanes(lax.rem(z + k + 1, NZ) * SUB, SUB)]


def dpre_kernel(own, e, mask, norm_row, act_hbm, w_dec, out, act, buf, act_sem, sems):
    c = lax.axis_index("c")
    copies = fetch_dec(w_dec, c, buf.at[0], sems) + fetch_dec(w_dec, 1 - c, buf.at[1], sems, 4)
    fetch = pltpu.make_async_copy(act_hbm, act, act_sem)
    fetch.start()
    both = e[:, HALF:].astype(f32) + own[:, HALF:].astype(f32)
    both = jnp.sum(jnp.sum(both, axis=0, keepdims=True), axis=1, keepdims=True)
    lane = lax.broadcasted_iota(jnp.int32, (8, LOCAL), 1)
    tail = jnp.zeros((8, LOCAL), f32)
    for i, piece in enumerate(split3(both)):
        tail = jnp.where(lane == i, piece.astype(f32), tail)
    out[ROWS:, :] = tail.astype(bf16)
    live = mask[:, 0:1].astype(f32)
    totals = [jnp.zeros((ROWS, 256), f32), jnp.zeros((ROWS, 256), f32)]
    for q in range(2 * NZ):
        copies[q].wait()
        rows = (own, e)[q // NZ]
        for i in range(2):
            totals[i] = totals[i] + lax.dot_general(
                rows[:, (q % NZ) * SUB : (q % NZ + 1) * SUB],
                buf[q // NZ, q % NZ, i * 256 : (i + 1) * 256, :],
                (((1,), (1,)), ((), ())),
                preferred_element_type=f32,
            )
    fetch.wait()
    for i in range(2):
        n = slice(i * 256, (i + 1) * 256)
        nsum = norm_row[0:1, n] + norm_row[1:2, n]
        grad = 2.0 * totals[i] + sparsity_weight * live * nsum
        out[:ROWS, n] = (grad * 2.0 * act[:, n]).astype(bf16)


def merge_kernel(a, b, d, out):
    for k, v in enumerate((a, b, d)):
        out[k * ROWS : (k + 1) * ROWS, :] = v[...]


def part_kernel(*refs):
    pres, slices, count = refs[0:4], refs[4:7], refs[7]
    es, loss = refs[8:]
    total = jnp.zeros((1, 1), f32)
    for p in pres:
        total = total + jnp.sum(p[ROWS : ROWS + 1, 0:3].astype(f32), axis=1, keepdims=True)
    for k, p in enumerate(slices):
        es[k * ROWS : (k + 1) * ROWS, :] = p[...]
    loss[...] = total / (count[0:1, 0:1] * WIDTH)


def dec_half(side, plane, rest, ft, scale, w, factor, done, out, sems):
    z = lax.axis_index("z")
    copies = []
    for i, m in enumerate(range(0, SUB, 512)):
        cols = lanes(side * SUB + m, 512)
        part = jnp.dot(ft[:, :ROWS], plane[:, lanes(z * SUB + m, 512)], preferred_element_type=f32)
        part = part + jnp.dot(ft[:, ROWS:], rest[:, m : m + 512], preferred_element_type=f32)
        part = part * (2.0 * factor) + (scale[...] * factor) * w[:, cols].astype(f32)
        done[i] = part.astype(bf16)
        copies.append(pltpu.make_async_copy(done.at[i], out.at[:, cols], sems[i]))
        copies[-1].start()
    return copies


def grads_kernel(xt, count, p0, p1, p2, p3, e_own, own, ft, scale, w, out_enc, out_dec, ds, done, done_dec, sems):
    for k, p in enumerate((p0, p1, p2, p3)):
        ds[k * ROWS : (k + 1) * ROWS, :] = p[:ROWS, :]
    factor = loss_scale / count[0:1, 0:1]
    copies = []
    for i in range(4):
        rows = pl.ds(i % 2 * 512, 512)
        part = jnp.dot(xt[i // 2, rows, :], ds[...], preferred_element_type=f32)
        done[i // 2, rows, :] = (part * factor).astype(bf16)
        copies.append(pltpu.make_async_copy(done.at[i // 2, rows], out_enc.at[i // 2, rows], sems.at[i]))
        copies[-1].start()
    copies += dec_half(
        lax.axis_index("c"), e_own, own, ft, scale, w, factor, done_dec, out_dec, [sems.at[4], sems.at[5]]
    )
    for copy in copies:
        copy.wait()


def rest_kernel(e_other, other, ft, scale, count, w, half, out, done, sems):
    del half
    side = 1 - lax.axis_index("c")
    factor = loss_scale / count[0:1, 0:1]
    for copy in dec_half(side, e_other, other, ft, scale, w, factor, done, out, [sems.at[0], sems.at[1]]):
        copy.wait()


def swap(v):
    return lax.ppermute(v, "c", [(0, 1), (1, 0)])


def chips(v):
    return lax.all_to_all(v, ("x", "y"), split_axis=0, concat_axis=0, tiled=True)


def planes(v):
    return lax.all_to_all(v, "z", split_axis=0, concat_axis=0, tiled=True)


def shift(v, k):
    return lax.ppermute(v, "z", [(i, (i + k) % NZ) for i in range(NZ)])


def shards(acts, chat_len, group_of, w_enc, b_enc, w_dec, b_dec):
    half_flops = 2 * ROWS * HALF * LOCAL
    w_enc, w_dec = at_hbm(w_enc), at_hbm(w_dec)
    dec_scratch = [pltpu.VMEM((4, LOCAL, SUB), bf16), pltpu.SemaphoreType.DMA((4,))]
    hbm = pl.BlockSpec(memory_space=pltpu.HBM)
    anywhere = pl.BlockSpec(memory_space=pl.ANY)
    keep, send = call(
        prep_kernel,
        [((4, 2 * HALF + PAD), bf16)] * 2,
        (chat_len, at_hbm(acts), at_hbm(group_of.reshape(1, 5))),
        [pl.BlockSpec(memory_space=pltpu.SMEM), hbm, hbm],
        [
            pltpu.VMEM((5, WIDTH), bf16),
            pltpu.VMEM((1, 5), jnp.int32),
            pltpu.SemaphoreType.DMA((2,)),
        ],
        vmem=4 * MIB,
    )
    block, mine = call(
        join_kernel,
        [((CHIPS, 8, HALF + PAD), bf16), ((8, HALF + PAD), bf16)],
        (keep, swap(send)),
        vmem=4 * MIB,
    )
    x_own = chips(block).reshape(ROWS, HALF + PAD)
    x_other = swap(x_own)
    acc, w_rest, mask, home_own, *xs = call(
        encode_own_kernel,
        [((ROWS, LOCAL), f32), ((HALF, LOCAL), bf16, pltpu.VMEM), ((ROWS, PAD), bf16)]
        + [((ROWS, SUB), bf16, pltpu.HBM)] * 4,
        (x_own, w_enc),
        [VM, hbm],
        [pltpu.VMEM((HALF, LOCAL), bf16), pltpu.SemaphoreType.DMA((8,)), pltpu.SemaphoreType.DMA((4,))],
        out_specs=[VM] * 3 + [hbm] * 4,
        flops=half_flops,
        nbytes=10 * MIB,
    )
    act, feats, part_send, home_other = call(
        encode_kernel,
        [
            ((ROWS, LOCAL), f32, pltpu.HBM),
            ((ROWS + 8, LOCAL), bf16),
            ((ROWS, HALF), bf16),
            ((ROWS, SUB), bf16, pltpu.HBM),
        ],
        (x_other, mask, acc, b_enc.reshape(1, LOCAL), w_rest, w_dec),
        [VM] * 5 + [hbm],
        [pltpu.VMEM((ROWS, LOCAL), f32), *dec_scratch, pltpu.SemaphoreType.DMA((2,))],
        out_specs=[hbm, VM, VM, hbm],
        flops=2 * half_flops,
        nbytes=8 * MIB,
    )
    part_recv = swap(part_send)
    (part_own,) = call(
        decode_own_kernel,
        [((ROWS, HALF), f32)],
        (feats, w_dec),
        [VM, hbm],
        dec_scratch,
        flops=half_flops,
        nbytes=6 * MIB,
    )
    (part,) = call(
        add_kernel,
        [((ROWS, HALF), bf16, pltpu.HBM)],
        (part_own, part_recv),
        scratch=[pltpu.VMEM((ROWS, HALF), bf16), pltpu.SemaphoreType.DMA((4,))],
        out_specs=[hbm],
        vmem=8 * MIB,
    )
    norm_row, norm_col = call(
        norm_kernel,
        [((2, LOCAL), f32), ((LOCAL, 2), f32)],
        (w_dec,),
        [hbm],
        [pltpu.VMEM((LOCAL, WIDTH), bf16), pltpu.SemaphoreType.DMA((4,))],
        flops=4 * LOCAL * WIDTH,
        nbytes=8 * MIB,
    )
    parts, norm_row, norm_col = lax.optimization_barrier((chips(part.reshape(CHIPS, 8, HALF)), norm_row, norm_col))
    xs = [shift(xs[k - 1], k) for k in range(1, NZ)]
    (block,) = call(
        err_kernel,
        [((CHIPS, 8, HALF + PAD), bf16, pltpu.HBM)],
        (parts, mine, b_dec, feats, norm_row),
        scratch=[pltpu.VMEM((CHIPS, 8, HALF + PAD), bf16), pltpu.SemaphoreType.DMA((NZ + 1,))],
        out_specs=[hbm],
    )
    block, *xs = lax.optimization_barrier((block, *xs))
    (xs,) = call(merge_kernel, [((3 * ROWS, SUB), bf16)], xs, nbytes=2 * MIB)
    fs = [feats] + [shift(feats, k) for k in range(1, NZ)]
    e_own, xs, xs_other, *fs = lax.optimization_barrier((chips(block), xs, swap(xs), *fs))
    e_own = e_own.reshape(ROWS, HALF + PAD)
    e_other = swap(e_own)
    slices = call(slice_kernel, [((ROWS, SUB), bf16)] * 3, (e_own,), nbytes=MIB)
    es = [shift(slices[k - 1], k) for k in range(1, NZ)]
    (dpre,) = call(
        dpre_kernel,
        [((ROWS + 8, LOCAL), bf16)],
        (e_own, e_other, mask, norm_row, at_hbm(act), w_dec),
        [VM] * 4 + [hbm] * 2,
        [
            pltpu.VMEM((ROWS, LOCAL), f32),
            pltpu.VMEM((2, NZ, LOCAL, SUB), bf16),
            pltpu.SemaphoreType.DMA,
            pltpu.SemaphoreType.DMA((8,)),
        ],
        flops=2 * half_flops,
        nbytes=10 * MIB,
    )
    ds = [dpre] + [shift(dpre, k) for k in range(1, NZ)]
    xt, ft, scale, count, w_slice = call(
        turn_kernel,
        [
            ((2, SUB, NZ * ROWS), bf16),
            ((LOCAL, NZ * ROWS), bf16),
            ((LOCAL, 1), f32),
            ((8, PAD), f32, pltpu.VMEM),
            ((LOCAL, 2 * SUB), bf16),
        ],
        (home_own, home_other, xs, xs_other, *fs, norm_col, w_dec, dpre),
        [VM] * 9 + [hbm, anywhere],
        [pltpu.SemaphoreType.DMA],
        nbytes=6 * MIB,
    )
    es, loss = call(
        part_kernel,
        [((3 * ROWS, SUB), bf16), ((1, 1), f32)],
        (*ds, *es, count),
        nbytes=3 * MIB,
    )
    grad_enc, half = call(
        grads_kernel,
        [((2, SUB, LOCAL), bf16), ((LOCAL, 2 * SUB), bf16)],
        (xt, count, *ds, e_own, es, ft, scale, w_slice),
        scratch=[
            pltpu.VMEM((NZ * ROWS, LOCAL), bf16),
            pltpu.VMEM((2, SUB, LOCAL), bf16),
            pltpu.VMEM((2, LOCAL, 512), bf16),
            pltpu.SemaphoreType.DMA((6,)),
        ],
        out_specs=[hbm, hbm],
        flops=6 * half_flops,
        nbytes=8 * MIB,
    )
    (grad_dec,) = call(
        rest_kernel,
        [((LOCAL, 2 * SUB), bf16)],
        (e_other, swap(es), ft, scale, count, w_slice, half),
        [VM] * 6 + [hbm],
        [pltpu.VMEM((2, LOCAL, 512), bf16), pltpu.SemaphoreType.DMA((2,))],
        out_specs=[hbm],
        aliases={6: 0},
        flops=2 * half_flops,
        nbytes=3 * MIB,
    )
    return grad_enc, grad_dec, loss.reshape(())


def solution(mesh):
    fine = Mesh(mesh.devices.reshape(4, 4, 4, 2), ALL)
    lat = ("x", "y", "c")
    return jax.shard_map(
        shards,
        mesh=fine,
        in_specs=(P(ALL, None), P(ALL), P(ALL, None), P(None, None, lat), P(lat), P(lat, None), P()),
        out_specs=(P(None, "z", lat), P(lat, "z"), P()),
        check_vma=False,
    )
```

```python
import jax
import jax.numpy as jnp
from jax import lax
from jax.experimental import pallas as pl
from jax.experimental.pallas import tpu as pltpu
from jax.sharding import Mesh
from jax.sharding import PartitionSpec as P

sparsity_weight = 1.0
loss_scale = 8.0
norm_eps = 1e-06

ALL = ("z", "x", "y", "c")
NZ = 4
CHIPS = 16
WIDTH = 8192
HALF = 4096
SUB = 1024
LOCAL = 512
ROWS = 128
PAD = 128
MIB = 1 << 20
f32 = jnp.float32
bf16 = jnp.bfloat16

VM = pl.BlockSpec(memory_space=pltpu.VMEM)


def at_hbm(v):
    return pltpu.with_memory_space_constraint(v, pltpu.HBM)


def call(body, outs, args, specs=None, scratch=(), vmem=None, flops=0, nbytes=0, out_specs=None, aliases=None):
    return pl.pallas_call(
        body,
        out_shape=[o[2](o[0], o[1]) if len(o) == 3 else jax.ShapeDtypeStruct(*o) for o in outs],
        in_specs=specs or [VM] * len(args),
        out_specs=out_specs or [VM] * len(outs),
        scratch_shapes=list(scratch),
        input_output_aliases=aliases or {},
        compiler_params=pltpu.CompilerParams(vmem_limit_bytes=vmem or 16 * MIB),
        cost_estimate=pl.CostEstimate(flops=flops, bytes_accessed=nbytes, transcendentals=0),
    )(*args)


def lanes(start, size):
    return pl.ds(pl.multiple_of(start, 128), size)


def split3(v):
    hi = v.astype(bf16)
    rest = v - hi.astype(f32)
    mid = rest.astype(bf16)
    low = (rest - mid.astype(f32)).astype(bf16)
    return hi, mid, low


def prep_kernel(length, acts_hbm, group_hbm, keep, send, acts, group, sems):
    copies = [
        pltpu.make_async_copy(src, dst, sems.at[i])
        for i, (src, dst) in enumerate(((acts_hbm, acts), (group_hbm, group)))
    ]
    for copy in copies:
        copy.start()
    for copy in copies:
        copy.wait()
    c = lax.axis_index("c")
    slot = lax.broadcasted_iota(jnp.int32, (1, 5), 1)
    held = jnp.sum(jnp.where(group[...] == NZ, slot, 0), axis=1, keepdims=True)
    k = lax.broadcasted_iota(jnp.int32, (4, 1), 0)
    later = k >= held
    src = k + later.astype(jnp.int32)
    live = (src < length[0]).astype(f32)
    live = jnp.broadcast_to(live, (4, PAD)).astype(bf16)

    def pick(cols):
        rows = acts[:, cols].astype(f32)
        return jnp.where(later, rows[1:5], rows[0:4]).astype(bf16)

    for out, core in ((keep, c), (send, 1 - c)):
        out[:, :HALF] = pick(lanes(core * HALF, HALF))
        for q in range(NZ):
            out[:, HALF + q * SUB : HALF + (q + 1) * SUB] = pick(lanes(q * 2 * SUB + core * SUB, SUB))
        out[:, 2 * HALF :] = live


def join_kernel(own, other, out, mine):
    first = lax.axis_index("c") == 0
    a, b = own[...].astype(f32), other[...].astype(f32)
    rows = jnp.concatenate([jnp.where(first, a, b), jnp.where(first, b, a)], axis=0)
    mine[...] = rows[:, HALF:].astype(bf16)
    for i in range(CHIPS):
        out[i, :, :HALF] = rows[:, :HALF].astype(bf16)
        out[i, :, HALF:] = rows[:, 2 * HALF :].astype(bf16)


def norm_kernel(w_dec_hbm, norm_row, norm_col, w_dec, sems):
    rows = LOCAL // 4
    copies = [
        pltpu.make_async_copy(w_dec_hbm.at[pl.ds(i * rows, rows)], w_dec.at[pl.ds(i * rows, rows)], sems.at[i])
        for i in range(4)
    ]
    for copy in copies:
        copy.start()
    for i in range(4):
        copies[i].wait()
        n = i * rows
        for s in range(2):

            def add(j, total):
                for m in range(4):
                    v = w_dec[n : n + rows, lanes(s * HALF + j * 512 + m * 128, 128)].astype(f32)
                    total = total + v * v
                return total

            total = lax.fori_loop(0, HALF // 512, add, jnp.zeros((rows, 128), f32))
            norm_row[s : s + 1, n : n + rows] = jnp.sqrt(jnp.sum(total.T, axis=0, keepdims=True) + norm_eps)
            norm_col[n : n + rows, s : s + 1] = jnp.sqrt(jnp.sum(total, axis=1, keepdims=True) + norm_eps)


def fetch_enc(w_hbm, core, buf, sems, at=0):
    copies = [
        pltpu.make_async_copy(w_hbm.at[core, pl.ds(i * SUB, SUB)], buf.at[pl.ds(i * SUB, SUB)], sems.at[at + i])
        for i in range(4)
    ]
    for copy in copies:
        copy.start()
    return copies


def fetch_dec(w_hbm, core, buf, sems, at=0):
    copies = [
        pltpu.make_async_copy(w_hbm.at[:, lanes(q * 2 * SUB + core * SUB, SUB)], buf.at[q], sems.at[at + q])
        for q in range(NZ)
    ]
    for copy in copies:
        copy.start()
    return copies


def encode_own_kernel(x, w_enc, acc, rest, mask, home, p1, p2, p3, buf, sems, out_sems):
    z, c = lax.axis_index("z"), lax.axis_index("c")
    copies = fetch_enc(w_enc, c, buf, sems)
    later = fetch_enc(w_enc, 1 - c, rest, sems, 4)
    for k, out in enumerate((home, p1, p2, p3)):
        piece = x.at[:, lanes(lax.rem(z + k, NZ) * SUB, SUB)]
        later.append(pltpu.make_async_copy(piece, out, out_sems.at[k]))
        later[-1].start()
    mask[...] = x[:, HALF:]
    for i in range(0, 4, 2):
        copies[i].wait()
        copies[i + 1].wait()
        rows = slice(i * SUB, (i + 2) * SUB)
        for n in range(0, LOCAL, 256):
            part = jnp.dot(x[:, rows], buf[rows, n : n + 256], preferred_element_type=f32)
            acc[:, n : n + 256] = part if i == 0 else acc[:, n : n + 256] + part
    for copy in later:
        copy.wait()


def encode_kernel(x, mask, part, bias, w_enc, w_dec, act_hbm, feats_out, send, home, act_out, dec, dec_sems, out_sems):
    z, c = lax.axis_index("z"), lax.axis_index("c")
    dec_copies = fetch_dec(w_dec, 1 - c, dec, dec_sems)
    later = [pltpu.make_async_copy(x.at[:, lanes(z * SUB, SUB)], home, out_sems.at[0])]
    later[0].start()
    live = mask[:, 0:1].astype(f32)
    count = jnp.sum(live, axis=0, keepdims=True)
    for n in range(0, LOCAL, 256):
        pre = part[:, n : n + 256] + jnp.dot(x[:, :HALF], w_enc[:, n : n + 256], preferred_element_type=f32)
        act = jnp.maximum(pre + bias[:, n : n + 256], 0.0)
        feats = act * act
        act_out[:, n : n + 256] = act
        feats_out[:ROWS, n : n + 256] = feats.astype(bf16)
        fsum = jnp.sum(feats * live, axis=0, keepdims=True)
        tail = jnp.zeros((8, 256), f32)
        row = lax.broadcasted_iota(jnp.int32, (8, 256), 0)
        for i, piece in enumerate((*split3(fsum), jnp.broadcast_to(count, (1, 256)))):
            tail = jnp.where(row == i, piece.astype(f32), tail)
        feats_out[ROWS:, n : n + 256] = tail.astype(bf16)
    later.append(pltpu.make_async_copy(act_out, act_hbm, out_sems.at[1]))
    later[1].start()
    feats16 = feats_out[:ROWS, :]
    for q in range(NZ):
        dec_copies[q].wait()
        send[:, q * SUB : (q + 1) * SUB] = jnp.dot(feats16, dec[q], preferred_element_type=f32).astype(bf16)
    for copy in later:
        copy.wait()


def decode_own_kernel(feats, w_dec, part, buf, sems):
    copies = fetch_dec(w_dec, lax.axis_index("c"), buf, sems)
    feats16 = feats[:ROWS, :]
    for q in range(NZ):
        copies[q].wait()
        part[:, q * SUB : (q + 1) * SUB] = jnp.dot(feats16, buf[q], preferred_element_type=f32)


def turn_kernel(home_own, home_other, own, other, *refs):
    z, c = lax.axis_index("z"), lax.axis_index("c")
    feats, norm_col, w_dec = refs[0:4], refs[4], refs[5]
    xt, ft, scale, count, w, sem = refs[7:]
    fetch = pltpu.make_async_copy(w_dec.at[:, lanes(z * 2 * SUB, 2 * SUB)], w, sem)
    fetch.start()
    fsum = jnp.zeros((1, LOCAL), f32)
    total = jnp.zeros((1, 1), f32)
    for side, mine, rest in ((c, home_own, own), (1 - c, home_other, other)):
        xt[side, :, :ROWS] = mine[...].T
        for k in range(1, NZ):
            xt[side, :, k * ROWS : (k + 1) * ROWS] = rest[(k - 1) * ROWS : k * ROWS, :].T
    for k in range(NZ):
        ft[:, k * ROWS : (k + 1) * ROWS] = feats[k][:ROWS, :].T
        fsum = fsum + jnp.sum(feats[k][ROWS : ROWS + 3, :].astype(f32), axis=0, keepdims=True)
        total = total + feats[k][ROWS + 3 : ROWS + 4, 0:1].astype(f32)
    count[...] = jnp.broadcast_to(total, (8, PAD))
    fsum = jnp.broadcast_to(fsum, (128, LOCAL)).T[:, 0:1]
    norm = jnp.where(z < 2, norm_col[:, 0:1], norm_col[:, 1:2])
    scale[...] = sparsity_weight * fsum / norm
    fetch.wait()


def add_kernel(own, other, out, total, sems):
    copies = []
    for i in range(4):
        rows = slice(i * 32, (i + 1) * 32)
        total[rows, :] = (own[rows, :] + other[rows, :].astype(f32)).astype(bf16)
        copies.append(pltpu.make_async_copy(total.at[pl.ds(i * 32, 32)], out.at[pl.ds(i * 32, 32)], sems.at[i]))
        copies[-1].start()
    for copy in copies:
        copy.wait()


def err_kernel(parts, mine, bias, feats, norm_row, out_hbm, out, sems):
    c = lax.axis_index("c")
    live = mine[:, HALF : HALF + 1].astype(f32)
    square = jnp.zeros((8, SUB), f32)
    copies = []
    for q in range(NZ):
        cols = slice(q * SUB, (q + 1) * SUB)
        total = parts[0, :, cols].astype(f32)
        for i in range(1, CHIPS):
            total = total + parts[i, :, cols].astype(f32)
        add = bias[q // 2 : q // 2 + 1, lanes((q % 2) * 2 * SUB + c * SUB, SUB)]
        err = (total + add - mine[:, cols].astype(f32)) * live
        square = square + err * err
        err16 = err.astype(bf16)
        for i in range(CHIPS):
            out[i, :, cols] = err16
        piece = pl.ds(q * SUB, SUB)
        copies.append(pltpu.make_async_copy(out.at[:, :, piece], out_hbm.at[:, :, piece], sems.at[q]))
        copies[-1].start()
    squares = jnp.sum(jnp.sum(square, axis=0, keepdims=True), axis=1, keepdims=True)
    fsum = jnp.sum(feats[ROWS : ROWS + 3, :].astype(f32), axis=0, keepdims=True)
    nsum = norm_row[0:1, :] + norm_row[1:2, :]
    sparse = sparsity_weight * jnp.sum(fsum * nsum, axis=1, keepdims=True)
    lane = lax.broadcasted_iota(jnp.int32, (8, PAD), 1)
    row = lax.broadcasted_iota(jnp.int32, (8, PAD), 0)
    tail = jnp.zeros((8, PAD), f32)
    for i, piece in enumerate(split3(squares + sparse)):
        tail = jnp.where((lane == i) & (row == 0), piece.astype(f32), tail)
    for i in range(CHIPS):
        out[i, :, HALF:] = tail.astype(bf16)
    piece = pl.ds(HALF, PAD)
    copies.append(pltpu.make_async_copy(out.at[:, :, piece], out_hbm.at[:, :, piece], sems.at[NZ]))
    copies[-1].start()
    for copy in copies:
        copy.wait()


def slice_kernel(e, s1, s2, s3):
    z = lax.axis_index("z")
    for k, out in enumerate((s1, s2, s3)):
        out[...] = e[:, lanes(lax.rem(z + k + 1, NZ) * SUB, SUB)]


def dpre_kernel(own, e, mask, norm_row, act_hbm, w_dec, out, act, buf, act_sem, sems):
    c = lax.axis_index("c")
    copies = fetch_dec(w_dec, c, buf.at[0], sems) + fetch_dec(w_dec, 1 - c, buf.at[1], sems, 4)
    fetch = pltpu.make_async_copy(act_hbm, act, act_sem)
    fetch.start()
    both = e[:, HALF:].astype(f32) + own[:, HALF:].astype(f32)
    both = jnp.sum(jnp.sum(both, axis=0, keepdims=True), axis=1, keepdims=True)
    lane = lax.broadcasted_iota(jnp.int32, (8, LOCAL), 1)
    tail = jnp.zeros((8, LOCAL), f32)
    for i, piece in enumerate(split3(both)):
        tail = jnp.where(lane == i, piece.astype(f32), tail)
    out[ROWS:, :] = tail.astype(bf16)
    live = mask[:, 0:1].astype(f32)
    totals = [jnp.zeros((ROWS, 256), f32), jnp.zeros((ROWS, 256), f32)]
    for q in range(2 * NZ):
        copies[q].wait()
        rows = (own, e)[q // NZ]
        for i in range(2):
            totals[i] = totals[i] + lax.dot_general(
                rows[:, (q % NZ) * SUB : (q % NZ + 1) * SUB],
                buf[q // NZ, q % NZ, i * 256 : (i + 1) * 256, :],
                (((1,), (1,)), ((), ())),
                preferred_element_type=f32,
            )
    fetch.wait()
    for i in range(2):
        n = slice(i * 256, (i + 1) * 256)
        nsum = norm_row[0:1, n] + norm_row[1:2, n]
        grad = 2.0 * totals[i] + sparsity_weight * live * nsum
        out[:ROWS, n] = (grad * 2.0 * act[:, n]).astype(bf16)


def merge_kernel(a, b, d, *refs):
    out = refs[-1]
    for k, v in enumerate((a, b, d)):
        out[k * ROWS : (k + 1) * ROWS, :] = v[...]


def dec_half(side, plane, rest, ft, scale, w, factor, done, out, sems):
    z = lax.axis_index("z")
    copies = []
    for i, m in enumerate(range(0, SUB, 512)):
        cols = lanes(side * SUB + m, 512)
        part = jnp.dot(ft[:, :ROWS], plane[:, lanes(z * SUB + m, 512)], preferred_element_type=f32)
        part = part + jnp.dot(ft[:, ROWS:], rest[:, m : m + 512], preferred_element_type=f32)
        part = part * (2.0 * factor) + (scale[...] * factor) * w[:, cols].astype(f32)
        done[i] = part.astype(bf16)
        copies.append(pltpu.make_async_copy(done.at[i], out.at[:, cols], sems[i]))
        copies[-1].start()
    return copies


def grads_kernel(
    xt, count, p0, p1, p2, p3, e_own, own, ft, scale, w, out_enc, out_dec, loss, ds, done, done_dec, total, sems
):
    loss_sum = jnp.zeros((1, 1), f32)
    for k, p in enumerate((p0, p1, p2, p3)):
        ds[k * ROWS : (k + 1) * ROWS, :] = p[:ROWS, :]
        loss_sum = loss_sum + jnp.sum(p[ROWS : ROWS + 1, 0:3].astype(f32), axis=1, keepdims=True)
    total[...] = loss_sum / (count[0:1, 0:1] * WIDTH)
    copies = [pltpu.make_async_copy(total, loss, sems.at[6])]
    copies[0].start()
    factor = loss_scale / count[0:1, 0:1]
    for i in range(4):
        rows = pl.ds(i % 2 * 512, 512)
        part = jnp.dot(xt[i // 2, rows, :], ds[...], preferred_element_type=f32)
        done[i // 2, rows, :] = (part * factor).astype(bf16)
        copies.append(pltpu.make_async_copy(done.at[i // 2, rows], out_enc.at[i // 2, rows], sems.at[i]))
        copies[-1].start()
    copies += dec_half(
        lax.axis_index("c"), e_own, own, ft, scale, w, factor, done_dec, out_dec, [sems.at[4], sems.at[5]]
    )
    for copy in copies:
        copy.wait()


def rest_kernel(e_other, other, ft, scale, count, w, half, out, done, sems):
    del half
    side = 1 - lax.axis_index("c")
    factor = loss_scale / count[0:1, 0:1]
    for copy in dec_half(side, e_other, other, ft, scale, w, factor, done, out, [sems.at[0], sems.at[1]]):
        copy.wait()


def swap(v):
    return lax.ppermute(v, "c", [(0, 1), (1, 0)])


def chips(v):
    return lax.all_to_all(v, ("x", "y"), split_axis=0, concat_axis=0, tiled=True)


def planes(v):
    return lax.all_to_all(v, "z", split_axis=0, concat_axis=0, tiled=True)


def shift(v, k):
    return lax.ppermute(v, "z", [(i, (i + k) % NZ) for i in range(NZ)])


def shards(acts, chat_len, group_of, w_enc, b_enc, w_dec, b_dec):
    half_flops = 2 * ROWS * HALF * LOCAL
    w_enc, w_dec = at_hbm(w_enc), at_hbm(w_dec)
    dec_scratch = [pltpu.VMEM((4, LOCAL, SUB), bf16), pltpu.SemaphoreType.DMA((4,))]
    hbm = pl.BlockSpec(memory_space=pltpu.HBM)
    anywhere = pl.BlockSpec(memory_space=pl.ANY)
    keep, send = call(
        prep_kernel,
        [((4, 2 * HALF + PAD), bf16)] * 2,
        (chat_len, at_hbm(acts), at_hbm(group_of.reshape(1, 5))),
        [pl.BlockSpec(memory_space=pltpu.SMEM), hbm, hbm],
        [
            pltpu.VMEM((5, WIDTH), bf16),
            pltpu.VMEM((1, 5), jnp.int32),
            pltpu.SemaphoreType.DMA((2,)),
        ],
        vmem=4 * MIB,
    )
    block, mine = call(
        join_kernel,
        [((CHIPS, 8, HALF + PAD), bf16), ((8, HALF + PAD), bf16)],
        (keep, swap(send)),
        vmem=4 * MIB,
    )
    x_own = chips(block).reshape(ROWS, HALF + PAD)
    x_other = swap(x_own)
    acc, w_rest, mask, home_own, *xs = call(
        encode_own_kernel,
        [((ROWS, LOCAL), f32), ((HALF, LOCAL), bf16, pltpu.VMEM), ((ROWS, PAD), bf16)]
        + [((ROWS, SUB), bf16, pltpu.HBM)] * 4,
        (x_own, w_enc),
        [VM, hbm],
        [pltpu.VMEM((HALF, LOCAL), bf16), pltpu.SemaphoreType.DMA((8,)), pltpu.SemaphoreType.DMA((4,))],
        out_specs=[VM] * 3 + [hbm] * 4,
        flops=half_flops,
        nbytes=10 * MIB,
    )
    act, feats, part_send, home_other = call(
        encode_kernel,
        [
            ((ROWS, LOCAL), f32, pltpu.HBM),
            ((ROWS + 8, LOCAL), bf16),
            ((ROWS, HALF), bf16),
            ((ROWS, SUB), bf16, pltpu.HBM),
        ],
        (x_other, mask, acc, b_enc.reshape(1, LOCAL), w_rest, w_dec),
        [VM] * 5 + [hbm],
        [pltpu.VMEM((ROWS, LOCAL), f32), *dec_scratch, pltpu.SemaphoreType.DMA((2,))],
        out_specs=[hbm, VM, VM, hbm],
        flops=2 * half_flops,
        nbytes=8 * MIB,
    )
    part_recv = swap(part_send)
    (part_own,) = call(
        decode_own_kernel,
        [((ROWS, HALF), f32)],
        (feats, w_dec),
        [VM, hbm],
        dec_scratch,
        flops=half_flops,
        nbytes=6 * MIB,
    )
    (part,) = call(
        add_kernel,
        [((ROWS, HALF), bf16, pltpu.HBM)],
        (part_own, part_recv),
        scratch=[pltpu.VMEM((ROWS, HALF), bf16), pltpu.SemaphoreType.DMA((4,))],
        out_specs=[hbm],
        vmem=8 * MIB,
    )
    norm_row, norm_col = call(
        norm_kernel,
        [((2, LOCAL), f32), ((LOCAL, 2), f32)],
        (w_dec,),
        [hbm],
        [pltpu.VMEM((LOCAL, WIDTH), bf16), pltpu.SemaphoreType.DMA((4,))],
        flops=4 * LOCAL * WIDTH,
        nbytes=8 * MIB,
    )
    parts, norm_row, norm_col = lax.optimization_barrier((chips(part.reshape(CHIPS, 8, HALF)), norm_row, norm_col))
    xs = [shift(xs[k - 1], k) for k in range(1, NZ)]
    (block,) = call(
        err_kernel,
        [((CHIPS, 8, HALF + PAD), bf16, pltpu.HBM)],
        (parts, mine, b_dec, feats, norm_row),
        scratch=[pltpu.VMEM((CHIPS, 8, HALF + PAD), bf16), pltpu.SemaphoreType.DMA((NZ + 1,))],
        out_specs=[hbm],
    )
    block, *xs = lax.optimization_barrier((block, *xs))
    (xs,) = call(merge_kernel, [((3 * ROWS, SUB), bf16)], xs, nbytes=2 * MIB)
    fs = [feats] + [shift(feats, k) for k in range(1, NZ)]
    e_own, xs, xs_other, *fs = lax.optimization_barrier((chips(block), xs, swap(xs), *fs))
    e_own = e_own.reshape(ROWS, HALF + PAD)
    e_other = swap(e_own)
    slices = call(slice_kernel, [((ROWS, SUB), bf16)] * 3, (e_own,), nbytes=MIB)
    es = [shift(slices[k - 1], k) for k in range(1, NZ)]
    (dpre,) = call(
        dpre_kernel,
        [((ROWS + 8, LOCAL), bf16)],
        (e_own, e_other, mask, norm_row, at_hbm(act), w_dec),
        [VM] * 4 + [hbm] * 2,
        [
            pltpu.VMEM((ROWS, LOCAL), f32),
            pltpu.VMEM((2, NZ, LOCAL, SUB), bf16),
            pltpu.SemaphoreType.DMA,
            pltpu.SemaphoreType.DMA((8,)),
        ],
        flops=2 * half_flops,
        nbytes=10 * MIB,
    )
    ds = [dpre] + [shift(dpre, k) for k in range(1, NZ)]
    xt, ft, scale, count, w_slice = call(
        turn_kernel,
        [
            ((2, SUB, NZ * ROWS), bf16),
            ((LOCAL, NZ * ROWS), bf16),
            ((LOCAL, 1), f32),
            ((8, PAD), f32, pltpu.VMEM),
            ((LOCAL, 2 * SUB), bf16),
        ],
        (home_own, home_other, xs, xs_other, *fs, norm_col, w_dec, dpre),
        [VM] * 9 + [hbm, anywhere],
        [pltpu.SemaphoreType.DMA],
        nbytes=6 * MIB,
    )
    (es,) = call(merge_kernel, [((3 * ROWS, SUB), bf16)], (*es, count, *ds[1:]), [VM] * 4 + [anywhere] * 3)
    grad_enc, half, loss = call(
        grads_kernel,
        [((2, SUB, LOCAL), bf16), ((LOCAL, 2 * SUB), bf16), ((1, 1), f32, pltpu.HBM)],
        (xt, count, *ds, e_own, es, ft, scale, w_slice),
        scratch=[
            pltpu.VMEM((NZ * ROWS, LOCAL), bf16),
            pltpu.VMEM((2, SUB, LOCAL), bf16),
            pltpu.VMEM((2, LOCAL, 512), bf16),
            pltpu.VMEM((1, 1), f32),
            pltpu.SemaphoreType.DMA((7,)),
        ],
        out_specs=[hbm] * 3,
        flops=6 * half_flops,
        nbytes=8 * MIB,
    )
    (grad_dec,) = call(
        rest_kernel,
        [((LOCAL, 2 * SUB), bf16)],
        (e_other, swap(es), ft, scale, count, w_slice, half),
        [VM] * 6 + [hbm],
        [pltpu.VMEM((2, LOCAL, 512), bf16), pltpu.SemaphoreType.DMA((2,))],
        out_specs=[hbm],
        aliases={6: 0},
        flops=2 * half_flops,
        nbytes=3 * MIB,
    )
    return grad_enc, grad_dec, loss.reshape(())


def solution(mesh):
    fine = Mesh(mesh.devices.reshape(4, 4, 4, 2), ALL)
    lat = ("x", "y", "c")
    return jax.shard_map(
        shards,
        mesh=fine,
        in_specs=(P(ALL, None), P(ALL), P(ALL, None), P(None, None, lat), P(lat), P(lat, None), P()),
        out_specs=(P(None, "z", lat), P(lat, "z"), P()),
        check_vma=False,
    )
```

```python
import jax
import jax.numpy as jnp
from jax import lax
from jax.experimental import pallas as pl
from jax.experimental.pallas import tpu as pltpu
from jax.sharding import Mesh
from jax.sharding import PartitionSpec as P

sparsity_weight = 1.0
loss_scale = 8.0
norm_eps = 1e-06

ALL = ("z", "x", "y", "c")
NZ = 4
CHIPS = 16
WIDTH = 8192
HALF = 4096
SUB = 1024
LOCAL = 512
ROWS = 128
PAD = 128
MIB = 1 << 20
f32 = jnp.float32
bf16 = jnp.bfloat16

VM = pl.BlockSpec(memory_space=pltpu.VMEM)


def at_hbm(v):
    return pltpu.with_memory_space_constraint(v, pltpu.HBM)


def call(body, outs, args, specs=None, scratch=(), vmem=None, flops=0, nbytes=0, out_specs=None, aliases=None):
    return pl.pallas_call(
        body,
        out_shape=[o[2](o[0], o[1]) if len(o) == 3 else jax.ShapeDtypeStruct(*o) for o in outs],
        in_specs=specs or [VM] * len(args),
        out_specs=out_specs or [VM] * len(outs),
        scratch_shapes=list(scratch),
        input_output_aliases=aliases or {},
        compiler_params=pltpu.CompilerParams(vmem_limit_bytes=vmem or 16 * MIB),
        cost_estimate=pl.CostEstimate(flops=flops, bytes_accessed=nbytes, transcendentals=0),
    )(*args)


def lanes(start, size):
    return pl.ds(pl.multiple_of(start, 128), size)


def split3(v):
    hi = v.astype(bf16)
    rest = v - hi.astype(f32)
    mid = rest.astype(bf16)
    low = (rest - mid.astype(f32)).astype(bf16)
    return hi, mid, low


def prep_kernel(length, acts_hbm, group_hbm, keep, send, acts, group, sems):
    copies = [
        pltpu.make_async_copy(src, dst, sems.at[i])
        for i, (src, dst) in enumerate(((acts_hbm, acts), (group_hbm, group)))
    ]
    for copy in copies:
        copy.start()
    for copy in copies:
        copy.wait()
    c = lax.axis_index("c")
    slot = lax.broadcasted_iota(jnp.int32, (1, 5), 1)
    held = jnp.sum(jnp.where(group[...] == NZ, slot, 0), axis=1, keepdims=True)
    k = lax.broadcasted_iota(jnp.int32, (4, 1), 0)
    later = k >= held
    src = k + later.astype(jnp.int32)
    live = (src < length[0]).astype(f32)
    live = jnp.broadcast_to(live, (4, PAD)).astype(bf16)

    def pick(cols):
        rows = acts[:, cols].astype(f32)
        return jnp.where(later, rows[1:5], rows[0:4]).astype(bf16)

    for out, core in ((keep, c), (send, 1 - c)):
        out[:, :HALF] = pick(lanes(core * HALF, HALF))
        for q in range(NZ):
            out[:, HALF + q * SUB : HALF + (q + 1) * SUB] = pick(lanes(q * 2 * SUB + core * SUB, SUB))
        out[:, 2 * HALF :] = live


def join_kernel(own, other, out, mine):
    first = lax.axis_index("c") == 0
    a, b = own[...].astype(f32), other[...].astype(f32)
    rows = jnp.concatenate([jnp.where(first, a, b), jnp.where(first, b, a)], axis=0)
    mine[...] = rows[:, HALF:].astype(bf16)
    for i in range(CHIPS):
        out[i, :, :HALF] = rows[:, :HALF].astype(bf16)
        out[i, :, HALF:] = rows[:, 2 * HALF :].astype(bf16)


def norm_kernel(w_dec_hbm, norm_row, norm_col, w_dec, sems):
    rows = LOCAL // 4
    copies = [
        pltpu.make_async_copy(w_dec_hbm.at[pl.ds(i * rows, rows)], w_dec.at[pl.ds(i * rows, rows)], sems.at[i])
        for i in range(4)
    ]
    for copy in copies:
        copy.start()
    for i in range(4):
        copies[i].wait()
        n = i * rows
        for s in range(2):

            def add(j, total):
                for m in range(4):
                    v = w_dec[n : n + rows, lanes(s * HALF + j * 512 + m * 128, 128)].astype(f32)
                    total = total + v * v
                return total

            total = lax.fori_loop(0, HALF // 512, add, jnp.zeros((rows, 128), f32))
            norm_row[s : s + 1, n : n + rows] = jnp.sqrt(jnp.sum(total.T, axis=0, keepdims=True) + norm_eps)
            norm_col[n : n + rows, s : s + 1] = jnp.sqrt(jnp.sum(total, axis=1, keepdims=True) + norm_eps)


def fetch_enc(w_hbm, core, buf, sems, at=0):
    copies = [
        pltpu.make_async_copy(w_hbm.at[core, pl.ds(i * SUB, SUB)], buf.at[pl.ds(i * SUB, SUB)], sems.at[at + i])
        for i in range(4)
    ]
    for copy in copies:
        copy.start()
    return copies


def fetch_dec(w_hbm, core, buf, sems, at=0):
    copies = [
        pltpu.make_async_copy(w_hbm.at[:, lanes(q * 2 * SUB + core * SUB, SUB)], buf.at[q], sems.at[at + q])
        for q in range(NZ)
    ]
    for copy in copies:
        copy.start()
    return copies


def encode_own_kernel(x, w_enc, acc, rest, mask, home, p1, p2, p3, buf, sems, out_sems):
    z, c = lax.axis_index("z"), lax.axis_index("c")
    copies = fetch_enc(w_enc, c, buf, sems)
    later = fetch_enc(w_enc, 1 - c, rest, sems, 4)
    for k, out in enumerate((home, p1, p2, p3)):
        piece = x.at[:, lanes(lax.rem(z + k, NZ) * SUB, SUB)]
        later.append(pltpu.make_async_copy(piece, out, out_sems.at[k]))
        later[-1].start()
    mask[...] = x[:, HALF:]
    for i in range(0, 4, 2):
        copies[i].wait()
        copies[i + 1].wait()
        rows = slice(i * SUB, (i + 2) * SUB)
        for n in range(0, LOCAL, 256):
            part = jnp.dot(x[:, rows], buf[rows, n : n + 256], preferred_element_type=f32)
            acc[:, n : n + 256] = part if i == 0 else acc[:, n : n + 256] + part
    for copy in later:
        copy.wait()


def encode_kernel(x, mask, part, bias, w_enc, w_dec, act_hbm, feats_out, send, home, act_out, dec, dec_sems, out_sems):
    z, c = lax.axis_index("z"), lax.axis_index("c")
    dec_copies = fetch_dec(w_dec, 1 - c, dec, dec_sems)
    later = [pltpu.make_async_copy(x.at[:, lanes(z * SUB, SUB)], home, out_sems.at[0])]
    later[0].start()
    live = mask[:, 0:1].astype(f32)
    count = jnp.sum(live, axis=0, keepdims=True)
    for n in range(0, LOCAL, 256):
        pre = part[:, n : n + 256] + jnp.dot(x[:, :HALF], w_enc[:, n : n + 256], preferred_element_type=f32)
        act = jnp.maximum(pre + bias[:, n : n + 256], 0.0)
        feats = act * act
        act_out[:, n : n + 256] = act
        feats_out[:ROWS, n : n + 256] = feats.astype(bf16)
        fsum = jnp.sum(feats * live, axis=0, keepdims=True)
        tail = jnp.zeros((8, 256), f32)
        row = lax.broadcasted_iota(jnp.int32, (8, 256), 0)
        for i, piece in enumerate((*split3(fsum), jnp.broadcast_to(count, (1, 256)))):
            tail = jnp.where(row == i, piece.astype(f32), tail)
        feats_out[ROWS:, n : n + 256] = tail.astype(bf16)
    later.append(pltpu.make_async_copy(act_out, act_hbm, out_sems.at[1]))
    later[1].start()
    feats16 = feats_out[:ROWS, :]
    for q in range(NZ):
        dec_copies[q].wait()
        send[:, q * SUB : (q + 1) * SUB] = jnp.dot(feats16, dec[q], preferred_element_type=f32).astype(bf16)
    for copy in later:
        copy.wait()


def decode_own_kernel(feats, w_dec, part, buf, sems):
    copies = fetch_dec(w_dec, lax.axis_index("c"), buf, sems)
    feats16 = feats[:ROWS, :]
    for q in range(NZ):
        copies[q].wait()
        part[:, q * SUB : (q + 1) * SUB] = jnp.dot(feats16, buf[q], preferred_element_type=f32)


def turn_kernel(home_own, home_other, own, other, *refs):
    z, c = lax.axis_index("z"), lax.axis_index("c")
    feats, norm_col, w_dec = refs[0:4], refs[4], refs[5]
    xt, ft, scale, count, w, sem = refs[7:]
    fetch = pltpu.make_async_copy(w_dec.at[:, lanes(z * 2 * SUB, 2 * SUB)], w, sem)
    fetch.start()
    fsum = jnp.zeros((1, LOCAL), f32)
    total = jnp.zeros((1, 1), f32)
    for side, mine, rest in ((c, home_own, own), (1 - c, home_other, other)):
        xt[side, :, :ROWS] = mine[...].T
        for k in range(1, NZ):
            xt[side, :, k * ROWS : (k + 1) * ROWS] = rest[(k - 1) * ROWS : k * ROWS, :].T
    for k in range(NZ):
        ft[:, k * ROWS : (k + 1) * ROWS] = feats[k][:ROWS, :].T
        fsum = fsum + jnp.sum(feats[k][ROWS : ROWS + 3, :].astype(f32), axis=0, keepdims=True)
        total = total + feats[k][ROWS + 3 : ROWS + 4, 0:1].astype(f32)
    count[...] = jnp.broadcast_to(total, (8, PAD))
    fsum = jnp.broadcast_to(fsum, (128, LOCAL)).T[:, 0:1]
    norm = jnp.where(z < 2, norm_col[:, 0:1], norm_col[:, 1:2])
    scale[...] = sparsity_weight * fsum / norm
    fetch.wait()


def add_kernel(own, other, out, total, sems):
    copies = []
    for i in range(4):
        rows = slice(i * 32, (i + 1) * 32)
        total[rows, :] = (own[rows, :] + other[rows, :].astype(f32)).astype(bf16)
        copies.append(pltpu.make_async_copy(total.at[pl.ds(i * 32, 32)], out.at[pl.ds(i * 32, 32)], sems.at[i]))
        copies[-1].start()
    for copy in copies:
        copy.wait()


def err_kernel(parts, mine, bias, feats, norm_row, out_hbm, out, sems):
    c = lax.axis_index("c")
    live = mine[:, HALF : HALF + 1].astype(f32)
    square = jnp.zeros((8, SUB), f32)
    copies = []
    for q in range(NZ):
        cols = slice(q * SUB, (q + 1) * SUB)
        total = parts[0, :, cols].astype(f32)
        for i in range(1, CHIPS):
            total = total + parts[i, :, cols].astype(f32)
        add = bias[q // 2 : q // 2 + 1, lanes((q % 2) * 2 * SUB + c * SUB, SUB)]
        err = (total + add - mine[:, cols].astype(f32)) * live
        square = square + err * err
        err16 = err.astype(bf16)
        for i in range(CHIPS):
            out[i, :, cols] = err16
        piece = pl.ds(q * SUB, SUB)
        copies.append(pltpu.make_async_copy(out.at[:, :, piece], out_hbm.at[:, :, piece], sems.at[q]))
        copies[-1].start()
    squares = jnp.sum(jnp.sum(square, axis=0, keepdims=True), axis=1, keepdims=True)
    fsum = jnp.sum(feats[ROWS : ROWS + 3, :].astype(f32), axis=0, keepdims=True)
    nsum = norm_row[0:1, :] + norm_row[1:2, :]
    sparse = sparsity_weight * jnp.sum(fsum * nsum, axis=1, keepdims=True)
    lane = lax.broadcasted_iota(jnp.int32, (8, PAD), 1)
    row = lax.broadcasted_iota(jnp.int32, (8, PAD), 0)
    tail = jnp.zeros((8, PAD), f32)
    for i, piece in enumerate(split3(squares + sparse)):
        tail = jnp.where((lane == i) & (row == 0), piece.astype(f32), tail)
    for i in range(CHIPS):
        out[i, :, HALF:] = tail.astype(bf16)
    piece = pl.ds(HALF, PAD)
    copies.append(pltpu.make_async_copy(out.at[:, :, piece], out_hbm.at[:, :, piece], sems.at[NZ]))
    copies[-1].start()
    for copy in copies:
        copy.wait()


def slice_kernel(e, s1, s2, s3):
    z = lax.axis_index("z")
    for k, out in enumerate((s1, s2, s3)):
        out[...] = e[:, lanes(lax.rem(z + k + 1, NZ) * SUB, SUB)]


def dpre_kernel(own, e, mask, norm_row, act_hbm, w_dec, out, act, buf, act_sem, sems):
    c = lax.axis_index("c")
    copies = fetch_dec(w_dec, c, buf.at[0], sems) + fetch_dec(w_dec, 1 - c, buf.at[1], sems, 4)
    fetch = pltpu.make_async_copy(act_hbm, act, act_sem)
    fetch.start()
    both = e[:, HALF:].astype(f32) + own[:, HALF:].astype(f32)
    both = jnp.sum(jnp.sum(both, axis=0, keepdims=True), axis=1, keepdims=True)
    lane = lax.broadcasted_iota(jnp.int32, (8, LOCAL), 1)
    tail = jnp.zeros((8, LOCAL), f32)
    for i, piece in enumerate(split3(both)):
        tail = jnp.where(lane == i, piece.astype(f32), tail)
    out[ROWS:, :] = tail.astype(bf16)
    live = mask[:, 0:1].astype(f32)
    totals = [jnp.zeros((ROWS, 256), f32), jnp.zeros((ROWS, 256), f32)]
    for q in range(2 * NZ):
        copies[q].wait()
        rows = (own, e)[q // NZ]
        for i in range(2):
            totals[i] = totals[i] + lax.dot_general(
                rows[:, (q % NZ) * SUB : (q % NZ + 1) * SUB],
                buf[q // NZ, q % NZ, i * 256 : (i + 1) * 256, :],
                (((1,), (1,)), ((), ())),
                preferred_element_type=f32,
            )
    fetch.wait()
    for i in range(2):
        n = slice(i * 256, (i + 1) * 256)
        nsum = norm_row[0:1, n] + norm_row[1:2, n]
        grad = 2.0 * totals[i] + sparsity_weight * live * nsum
        out[:ROWS, n] = (grad * 2.0 * act[:, n]).astype(bf16)


def merge_kernel(a, b, d, *refs):
    out = refs[-1]
    for k, v in enumerate((a, b, d)):
        out[k * ROWS : (k + 1) * ROWS, :] = v[...]


def dec_half(side, plane, rest, ft, scale, w, factor, done, out, sems):
    z = lax.axis_index("z")
    copies = []
    for i, m in enumerate(range(0, SUB, 256)):
        cols = lanes(side * SUB + m, 256)
        part = jnp.dot(ft[:, :ROWS], plane[:, lanes(z * SUB + m, 256)], preferred_element_type=f32)
        part = part + jnp.dot(ft[:, ROWS:], rest[:, m : m + 256], preferred_element_type=f32)
        part = part * (2.0 * factor) + (scale[...] * factor) * w[:, cols].astype(f32)
        done[i] = part.astype(bf16)
        copies.append(pltpu.make_async_copy(done.at[i], out.at[:, cols], sems[i]))
        copies[-1].start()
    return copies


def grads_kernel(
    xt, count, p0, p1, p2, p3, e_own, own, ft, scale, w, out_enc, out_dec, loss, ds, done, done_dec, total, sems
):
    loss_sum = jnp.zeros((1, 1), f32)
    for k, p in enumerate((p0, p1, p2, p3)):
        ds[k * ROWS : (k + 1) * ROWS, :] = p[:ROWS, :]
        loss_sum = loss_sum + jnp.sum(p[ROWS : ROWS + 1, 0:3].astype(f32), axis=1, keepdims=True)
    total[...] = loss_sum / (count[0:1, 0:1] * WIDTH)
    copies = [pltpu.make_async_copy(total, loss, sems.at[6])]
    copies[0].start()
    factor = loss_scale / count[0:1, 0:1]
    for i in range(4):
        rows = pl.ds(i % 2 * 512, 512)
        part = jnp.dot(xt[i // 2, rows, :], ds[...], preferred_element_type=f32)
        done[i // 2, rows, :] = (part * factor).astype(bf16)
        copies.append(pltpu.make_async_copy(done.at[i // 2, rows], out_enc.at[i // 2, rows], sems.at[i]))
        copies[-1].start()
    copies += dec_half(
        lax.axis_index("c"), e_own, own, ft, scale, w, factor, done_dec, out_dec, [sems.at[i] for i in (4, 5, 7, 8)]
    )
    for copy in copies:
        copy.wait()


def rest_kernel(e_other, other, ft, scale, count, w, half, out, done, sems):
    del half
    side = 1 - lax.axis_index("c")
    factor = loss_scale / count[0:1, 0:1]
    for copy in dec_half(side, e_other, other, ft, scale, w, factor, done, out, [sems.at[i] for i in range(4)]):
        copy.wait()


def swap(v):
    return lax.ppermute(v, "c", [(0, 1), (1, 0)])


def chips(v):
    return lax.all_to_all(v, ("x", "y"), split_axis=0, concat_axis=0, tiled=True)


def planes(v):
    return lax.all_to_all(v, "z", split_axis=0, concat_axis=0, tiled=True)


def shift(v, k):
    return lax.ppermute(v, "z", [(i, (i + k) % NZ) for i in range(NZ)])


def shards(acts, chat_len, group_of, w_enc, b_enc, w_dec, b_dec):
    half_flops = 2 * ROWS * HALF * LOCAL
    w_enc, w_dec = at_hbm(w_enc), at_hbm(w_dec)
    dec_scratch = [pltpu.VMEM((4, LOCAL, SUB), bf16), pltpu.SemaphoreType.DMA((4,))]
    hbm = pl.BlockSpec(memory_space=pltpu.HBM)
    anywhere = pl.BlockSpec(memory_space=pl.ANY)
    keep, send = call(
        prep_kernel,
        [((4, 2 * HALF + PAD), bf16)] * 2,
        (chat_len, at_hbm(acts), at_hbm(group_of.reshape(1, 5))),
        [pl.BlockSpec(memory_space=pltpu.SMEM), hbm, hbm],
        [
            pltpu.VMEM((5, WIDTH), bf16),
            pltpu.VMEM((1, 5), jnp.int32),
            pltpu.SemaphoreType.DMA((2,)),
        ],
        vmem=4 * MIB,
    )
    block, mine = call(
        join_kernel,
        [((CHIPS, 8, HALF + PAD), bf16), ((8, HALF + PAD), bf16)],
        (keep, swap(send)),
        vmem=4 * MIB,
    )
    x_own = chips(block).reshape(ROWS, HALF + PAD)
    x_other = swap(x_own)
    acc, w_rest, mask, home_own, *xs = call(
        encode_own_kernel,
        [((ROWS, LOCAL), f32), ((HALF, LOCAL), bf16, pltpu.VMEM), ((ROWS, PAD), bf16)]
        + [((ROWS, SUB), bf16, pltpu.HBM)] * 4,
        (x_own, w_enc),
        [VM, hbm],
        [pltpu.VMEM((HALF, LOCAL), bf16), pltpu.SemaphoreType.DMA((8,)), pltpu.SemaphoreType.DMA((4,))],
        out_specs=[VM] * 3 + [hbm] * 4,
        flops=half_flops,
        nbytes=10 * MIB,
    )
    act, feats, part_send, home_other = call(
        encode_kernel,
        [
            ((ROWS, LOCAL), f32, pltpu.HBM),
            ((ROWS + 8, LOCAL), bf16),
            ((ROWS, HALF), bf16),
            ((ROWS, SUB), bf16, pltpu.HBM),
        ],
        (x_other, mask, acc, b_enc.reshape(1, LOCAL), w_rest, w_dec),
        [VM] * 5 + [hbm],
        [pltpu.VMEM((ROWS, LOCAL), f32), *dec_scratch, pltpu.SemaphoreType.DMA((2,))],
        out_specs=[hbm, VM, VM, hbm],
        flops=2 * half_flops,
        nbytes=8 * MIB,
    )
    part_recv = swap(part_send)
    (part_own,) = call(
        decode_own_kernel,
        [((ROWS, HALF), f32)],
        (feats, w_dec),
        [VM, hbm],
        dec_scratch,
        flops=half_flops,
        nbytes=6 * MIB,
    )
    (part,) = call(
        add_kernel,
        [((ROWS, HALF), bf16, pltpu.HBM)],
        (part_own, part_recv),
        scratch=[pltpu.VMEM((ROWS, HALF), bf16), pltpu.SemaphoreType.DMA((4,))],
        out_specs=[hbm],
        vmem=8 * MIB,
    )
    norm_row, norm_col = call(
        norm_kernel,
        [((2, LOCAL), f32), ((LOCAL, 2), f32)],
        (w_dec,),
        [hbm],
        [pltpu.VMEM((LOCAL, WIDTH), bf16), pltpu.SemaphoreType.DMA((4,))],
        flops=4 * LOCAL * WIDTH,
        nbytes=8 * MIB,
    )
    parts, norm_row, norm_col = lax.optimization_barrier((chips(part.reshape(CHIPS, 8, HALF)), norm_row, norm_col))
    xs = [shift(xs[k - 1], k) for k in range(1, NZ)]
    (block,) = call(
        err_kernel,
        [((CHIPS, 8, HALF + PAD), bf16, pltpu.HBM)],
        (parts, mine, b_dec, feats, norm_row),
        scratch=[pltpu.VMEM((CHIPS, 8, HALF + PAD), bf16), pltpu.SemaphoreType.DMA((NZ + 1,))],
        out_specs=[hbm],
    )
    block, *xs = lax.optimization_barrier((block, *xs))
    (xs,) = call(merge_kernel, [((3 * ROWS, SUB), bf16)], xs, nbytes=2 * MIB)
    fs = [feats] + [shift(feats, k) for k in range(1, NZ)]
    e_own, xs, xs_other, *fs = lax.optimization_barrier((chips(block), xs, swap(xs), *fs))
    e_own = e_own.reshape(ROWS, HALF + PAD)
    e_other = swap(e_own)
    slices = call(slice_kernel, [((ROWS, SUB), bf16)] * 3, (e_own,), nbytes=MIB)
    es = [shift(slices[k - 1], k) for k in range(1, NZ)]
    (dpre,) = call(
        dpre_kernel,
        [((ROWS + 8, LOCAL), bf16)],
        (e_own, e_other, mask, norm_row, at_hbm(act), w_dec),
        [VM] * 4 + [hbm] * 2,
        [
            pltpu.VMEM((ROWS, LOCAL), f32),
            pltpu.VMEM((2, NZ, LOCAL, SUB), bf16),
            pltpu.SemaphoreType.DMA,
            pltpu.SemaphoreType.DMA((8,)),
        ],
        flops=2 * half_flops,
        nbytes=10 * MIB,
    )
    ds = [dpre] + [shift(dpre, k) for k in range(1, NZ)]
    xt, ft, scale, count, w_slice = call(
        turn_kernel,
        [
            ((2, SUB, NZ * ROWS), bf16),
            ((LOCAL, NZ * ROWS), bf16),
            ((LOCAL, 1), f32),
            ((8, PAD), f32, pltpu.VMEM),
            ((LOCAL, 2 * SUB), bf16),
        ],
        (home_own, home_other, xs, xs_other, *fs, norm_col, w_dec, dpre),
        [VM] * 9 + [hbm, anywhere],
        [pltpu.SemaphoreType.DMA],
        nbytes=6 * MIB,
    )
    (es,) = call(merge_kernel, [((3 * ROWS, SUB), bf16)], (*es, count, *ds[1:]), [VM] * 4 + [anywhere] * 3)
    grad_enc, half, loss = call(
        grads_kernel,
        [((2, SUB, LOCAL), bf16), ((LOCAL, 2 * SUB), bf16), ((1, 1), f32, pltpu.HBM)],
        (xt, count, *ds, e_own, es, ft, scale, w_slice),
        scratch=[
            pltpu.VMEM((NZ * ROWS, LOCAL), bf16),
            pltpu.VMEM((2, SUB, LOCAL), bf16),
            pltpu.VMEM((4, LOCAL, 256), bf16),
            pltpu.VMEM((1, 1), f32),
            pltpu.SemaphoreType.DMA((9,)),
        ],
        out_specs=[hbm] * 3,
        flops=6 * half_flops,
        nbytes=8 * MIB,
    )
    (grad_dec,) = call(
        rest_kernel,
        [((LOCAL, 2 * SUB), bf16)],
        (e_other, swap(es), ft, scale, count, w_slice, half),
        [VM] * 6 + [hbm],
        [pltpu.VMEM((4, LOCAL, 256), bf16), pltpu.SemaphoreType.DMA((4,))],
        out_specs=[hbm],
        aliases={6: 0},
        flops=2 * half_flops,
        nbytes=3 * MIB,
    )
    return grad_enc, grad_dec, loss.reshape(())


def solution(mesh):
    fine = Mesh(mesh.devices.reshape(4, 4, 4, 2), ALL)
    lat = ("x", "y", "c")
    return jax.shard_map(
        shards,
        mesh=fine,
        in_specs=(P(ALL, None), P(ALL), P(ALL, None), P(None, None, lat), P(lat), P(lat, None), P()),
        out_specs=(P(None, "z", lat), P(lat, "z"), P()),
        check_vma=False,
    )
```
